512 devices in a mesh: gx: 32 (over z, x_lo), gy: 16 (over x_hi, y, core).
Axes of the slice: x: 4 (x_hi: 2, x_lo: 2; x = x_hi * 2 + x_lo), y: 4, z: 16, core: 2. Of those that a mesh axis runs over, the one named last changes fastest.
Arguments:
- disp: float32 [2, 256, 16384], P(None, 'gx', 'gy'), may hold values from -0.2 to 0.2
- vel: float32 [2, 256, 16384], P(None, 'gx', 'gy'), may hold values from -1 to 1
- bonds: int32 [4, 256, 16384], P(None, 'gx', 'gy'), may hold values from 0 to 127, as said below
Outputs:
- new_disp: float32 [2, 256, 16384], P(None, 'gx', 'gy')
- new_vel: float32 [2, 256, 16384], P(None, 'gx', 'gy')
The draws below stay inside these ranges and needn't reach their ends.
Inputs may be any that keep to these rules, and one draw needn't show every extreme that they name: `bonds`: bit j of word 0 is bit j of the table's word 0 (j < 3), bits 0 to 6 of words 1 to 3 likewise; word 0 is below 8 and no higher bits are set.
All inputs are finite; a program needn't handle non-finite values.
Results may differ from the reference program's by a relative error of at most 0.00002.
Values sent between devices are 32-bit elements; how exact they have to be, the bound alone decides.
No kernel may reach another device: no remote copies, remote signals or barrier semaphores. Data moves between devices by JAX's collectives and lax.ppermute only.
A program may use at most 64 MiB of HBM per device.

```python
import math
import jax
import jax.numpy as jnp

STEPS = 2
NX = 256
NY = 16384


def draw_bonds(key, part):
    subkeys = jax.random.split(key, 3)
    grid_shape = (4, NX, NY)
    draw_one = jax.random.randint(subkeys[0], grid_shape, 0, 128)
    draw_two = jax.random.randint(subkeys[1], grid_shape, 0, 128)
    draw_three = jax.random.randint(subkeys[2], grid_shape, 0, 128)
    packed = jnp.bitwise_or(jnp.bitwise_or(draw_one, draw_two), draw_three)
    ceiling = jnp.where(jnp.arange(4)[:, None, None] == 0, 7, 127).astype(jnp.int32)
    return jnp.bitwise_and(packed, ceiling).astype(jnp.int32)


def level_of(rng, dims, cuts, least, high):
    factor_of = 1.0
    for dim, blocks in cuts:
        steps = jax.random.uniform(jax.random.fold_in(jax.random.fold_in(rng, 6), dim), (blocks,), jnp.float32, least / len(cuts), high / len(cuts))
        factor_of = factor_of * jnp.repeat(jnp.exp(steps), dims[dim] // blocks).reshape((-1,) + (1,) * (len(dims) - 1 - dim))
    return factor_of


def setup_inputs(seed: int = 0) -> dict:
    key_of = jax.random.split(jax.random.key(seed), 4)
    return {
        "disp": jnp.clip(jax.random.uniform(key_of[0], (2, NX, NY), jnp.float32, -0.2, 0.2) * level_of(key_of[0], (2, NX, NY), ((1, 32), (2, 16)), -0.4, 0.0), -0.2, 0.2),
        "vel": jnp.clip(jax.random.uniform(key_of[1], (2, NX, NY), jnp.float32, -1.0, 1.0) * level_of(key_of[1], (2, NX, NY), ((1, 32), (2, 16)), -0.4, 0.0), -1.0, 1.0),
        "bonds": draw_bonds(jax.random.fold_in(key_of[3], 71), 0),
    }


STIFFNESS = 40.0
DAMPING = 1.0
TIME_STEP = 0.05
SOFTENING = 0.0625
BOND_TABLE = [(0, c, 0, c - 1) for c in (1, 2, 3)] + [(r, c, r, c + 3) for r in (1, 2, 3) for c in (-3, -2, -1, 0, 1, 2, 3)]

def bond_force(near_state, far_state, row_off, col_off, intact):
    length = math.sqrt(row_off * row_off + col_off * col_off)
    rest = math.sqrt(length * length + SOFTENING)
    along_x = row_off + far_state[0] - near_state[0]
    along_y = col_off + far_state[1] - near_state[1]
    stretched = jnp.sqrt(along_x * along_x + along_y * along_y + SOFTENING)
    strain = (stretched - rest) / length
    closing = (along_x * (far_state[2] - near_state[2]) + along_y * (far_state[3] - near_state[3])) / (stretched * length)
    tension = intact * (STIFFNESS * strain + DAMPING * closing) / length
    return (tension * along_x / stretched, tension * along_y / stretched)

def intact_bits(word_array, bit):
    return jnp.bitwise_and(jnp.right_shift(word_array, bit), 1).astype(jnp.float32)

def total_force(state, bonds):
    force_x = jnp.zeros(state.shape[1:], jnp.float32)
    force_y = jnp.zeros(state.shape[1:], jnp.float32)
    for row_off, col_off, word, bit in BOND_TABLE:
        far_state = jnp.roll(state, (-row_off, -col_off), axis=(1, 2))
        pull_x, pull_y = bond_force(state, far_state, row_off, col_off, intact_bits(bonds[word], bit))
        force_x = force_x + pull_x - jnp.roll(pull_x, (row_off, col_off), axis=(0, 1))
        force_y = force_y + pull_y - jnp.roll(pull_y, (row_off, col_off), axis=(0, 1))
    return jnp.stack([force_x, force_y])

def reference(disp, vel, bonds):
    acceleration = total_force(jnp.concatenate([disp, vel], 0), bonds)
    for step in range(STEPS):
        half_vel = vel + 0.5 * TIME_STEP * acceleration
        disp = disp + TIME_STEP * half_vel
        acceleration = total_force(jnp.concatenate([disp, half_vel], 0), bonds)
        vel = half_vel + 0.5 * TIME_STEP * acceleration
    return (disp, vel)
```

```python
import math

import jax
import jax.numpy as jnp
from jax import lax
from jax.experimental import pallas as pl
from jax.experimental.pallas import tpu as pltpu
from jax.sharding import PartitionSpec as P

STIFFNESS = 40.0
TIME_STEP = 0.05
SOFTENING = 0.0625
PACK_SHIFT = (0, 3, 10, 17)
LANES = 128

ROWS = 8
PITCH = 9
BLOCK = ROWS * PITCH
FIELDS = 5
HALO = 9
GUARD = 8
LINES = 256


def row_line(row):
    return GUARD + PITCH * (row + HALO)


def lane_ids():
    return lax.broadcasted_iota(jnp.int32, (8, LANES), 1)


def pack_kernel(disp_ref, vel_ref, bonds_ref, edge_ref, block_ref):
    low_half = lane_ids() < LANES // 2
    for field in range(FIELDS):
        tiles = []
        for tile in range(ROWS):
            cols = pl.ds(tile * LANES, LANES)
            if field < 2:
                value = disp_ref[field, :, cols]
            elif field < 4:
                value = vel_ref[field - 2, :, cols]
            else:
                value = bonds_ref[0, :, cols]
                for word in (1, 2, 3):
                    value = value + bonds_ref[word, :, cols] * (1 << PACK_SHIFT[word])
                value = value.astype(jnp.float32)
            block_ref[pl.ds(field * BLOCK + tile + 1, ROWS, stride=PITCH), :] = value
            tiles.append(value)
        edge = jnp.where(low_half, tiles[0], tiles[-1])
        edge_ref[pl.ds(8 * field, 8), :] = edge
        block_ref[pl.ds(field * BLOCK, ROWS, stride=PITCH), :] = edge


def halo_kernel(parity_ref, block_in, even_ref, odd_ref, block_ref, first_ref, last_ref):
    low_half = lane_ids() < LANES // 2
    is_even = parity_ref[1] == 0
    block_ref[...] = block_in[...]
    for field in range(FIELDS):
        even = even_ref[pl.ds(8 * field, 8), :]
        odd = odd_ref[pl.ds(8 * field, 8), :]
        from_right = jnp.where(is_even, even, odd)
        from_left = jnp.where(is_even, odd, even)
        block_ref[pl.ds(field * BLOCK, ROWS, stride=PITCH), :] = jnp.where(
            low_half, from_right, from_left
        )
        first_ref[pl.ds(PITCH * field, PITCH), :] = block_ref[pl.ds(field * BLOCK, PITCH), :]
        last_ref[pl.ds(PITCH * field, PITCH), :] = block_ref[
            pl.ds(field * BLOCK + BLOCK - PITCH, PITCH), :
        ]


def shifted(here, after, before, by, lanes):
    if by > 0:
        return pltpu.roll(jnp.where(lanes < by, after, here), LANES - by, 1)
    if by < 0:
        return pltpu.roll(jnp.where(lanes >= LANES + by, before, here), -by, 1)
    return here


def force_lines(data, masks, push, pull, start, count, fresh_masks):
    lanes = lane_ids()

    def body(step, carry):
        line = start + 8 * step

        def at(field, offset):
            return data[field, pl.ds(line + offset, 8), :]

        here = [at(f, 0) for f in range(4)]
        after = [at(f, 1) for f in range(4)]
        before = [at(f, -1) for f in range(4)]
        near = []
        words = []
        for row_off in range(4):
            if row_off == 0:
                near.append(here)
            else:
                value = [at(f, -PITCH * row_off) for f in range(4)]
                value[0] = value[0] - float(row_off)
                near.append(value)
            if fresh_masks:
                words.append(at(4, -PITCH * row_off).astype(jnp.int32))
        own = [None] * 4
        for col_off in range(-3, 4):
            far = [shifted(here[f], after[f], before[f], col_off, lanes) for f in range(4)]
            if col_off:
                far[1] = far[1] + float(col_off)
            sum_x = sum_y = None
            for row_off in range(4):
                if row_off == 0 and col_off <= 0:
                    continue
                bit = col_off - 1 if row_off == 0 else col_off + 3
                slot = PACK_SHIFT[row_off] + bit
                squared = row_off * row_off + col_off * col_off
                rest = math.sqrt(squared + SOFTENING)
                base = near[row_off]
                along_x = far[0] - base[0]
                along_y = far[1] - base[1]
                rate_x = far[2] - base[2]
                rate_y = far[3] - base[3]
                inverse = lax.rsqrt(along_x * along_x + (along_y * along_y + SOFTENING))
                dot = along_x * rate_x + along_y * rate_y
                if fresh_masks:
                    mask = jnp.where((words[row_off] & (1 << slot)) != 0, 1.0 / squared, 0.0)
                    masks[slot, pl.ds(line, 8), :] = mask
                else:
                    mask = masks[slot, pl.ds(line, 8), :]
                scale = mask * (
                    STIFFNESS - (STIFFNESS * rest - dot * inverse) * inverse
                )
                pull_x = scale * along_x
                pull_y = scale * along_y
                sum_x = pull_x if sum_x is None else sum_x + pull_x
                sum_y = pull_y if sum_y is None else sum_y + pull_y
                if own[row_off] is None:
                    own[row_off] = (pull_x, pull_y)
                else:
                    own[row_off] = (own[row_off][0] + pull_x, own[row_off][1] + pull_y)
            push[2 * (col_off + 3), pl.ds(line, 8), :] = sum_x
            push[2 * (col_off + 3) + 1, pl.ds(line, 8), :] = sum_y
        for row_off in range(4):
            pull[2 * row_off, pl.ds(line, 8), :] = own[row_off][0]
            pull[2 * row_off + 1, pl.ds(line, 8), :] = own[row_off][1]
        return carry

    lax.fori_loop(0, count, body, 0)


def update_lines(data, push, pull, start, count, which):
    lanes = lane_ids()

    def body(step, carry):
        line = start + 8 * step
        for part in range(2):
            force = pull[part, pl.ds(line, 8), :]
            for row_off in (1, 2, 3):
                force = force + pull[2 * row_off + part, pl.ds(line + PITCH * row_off, 8), :]
            for col_off in range(-3, 4):
                slot = 2 * (col_off + 3) + part
                here = push[slot, pl.ds(line, 8), :]
                if col_off > 0:
                    here = shifted(here, None, push[slot, pl.ds(line - 1, 8), :], -col_off, lanes)
                elif col_off < 0:
                    here = shifted(here, push[slot, pl.ds(line + 1, 8), :], None, -col_off, lanes)
                force = force - here
            change = (0.5 * TIME_STEP) * force
            speed = data[2 + part, pl.ds(line, 8), :] + change
            if which == 1:
                speed = speed + change
            data[2 + part, pl.ds(line, 8), :] = speed
            if which < 2:
                data[part, pl.ds(line, 8), :] = (
                    data[part, pl.ds(line, 8), :] + TIME_STEP * speed
                )
        return carry

    lax.fori_loop(0, count, body, 0)


def step_kernel(
    parity_ref, block_ref, even_ref, odd_ref, below_ref, above_ref,
    disp_ref, vel_ref, data, masks, push, pull,
):
    lanes = lane_ids()
    low_half = lanes < LANES // 2
    is_even = parity_ref[0] == 0
    even_line = jnp.where(is_even, row_line(8), row_line(-8))
    odd_line = jnp.where(is_even, row_line(-8), row_line(8))
    for field in range(FIELDS):
        for part in range(PITCH):
            source = pl.ds(field * BLOCK + 8 * part, 8)
            data[field, pl.ds(row_line(0) + 8 * part, 8), :] = block_ref[source, :]
            data[field, pl.ds(even_line + 8 * part, 8), :] = even_ref[source, :]
            data[field, pl.ds(odd_line + 8 * part, 8), :] = odd_ref[source, :]
        ends = pl.ds(PITCH * field, PITCH)
        data[field, pl.ds(row_line(-9), PITCH), :] = below_ref[ends, :]
        data[field, pl.ds(row_line(16), PITCH), :] = above_ref[ends, :]
    for field in range(FIELDS):
        lines = [
            (row_line(-8) + 8 * PITCH * k, 8 if k < 3 else 2) for k in range(4)
        ]
        joined = []
        for line, size in lines:
            own = data[field, pl.ds(line, size, stride=PITCH), :]
            ahead = data[field, pl.ds(line - PITCH, size, stride=PITCH), :]
            joined.append(jnp.where(low_half[:size], ahead, own))
        for (line, size), value in zip(lines, joined):
            data[field, pl.ds(line, size, stride=PITCH), :] = value
    for which in range(3):
        reach = 3 * (2 - which)
        low, high = -reach, ROWS + reach
        first, last = row_line(low), row_line(high + 3) + 1
        force_lines(data, masks, push, pull, first, -(-(last - first) // 8), which == 0)
        last = row_line(high) + 1
        update_lines(data, push, pull, first, -(-(last - first) // 8), which)
    for tile in range(ROWS):
        lines = pl.ds(row_line(0) + 1 + tile, ROWS, stride=PITCH)
        cols = pl.ds(tile * LANES, LANES)
        for part in range(2):
            disp_ref[part, :, cols] = data[part, lines, :]
            vel_ref[part, :, cols] = data[2 + part, lines, :]


def shift(array, axis, by):
    count = lax.axis_size(axis)
    return lax.ppermute(array, axis, [(i, (i + by) % count) for i in range(count)])


def swap(array, axis, odd):
    count = lax.axis_size(axis)
    pairs = []
    for i in range(odd, count + odd, 2):
        pairs += [(i % count, (i + 1) % count), ((i + 1) % count, i % count)]
    return lax.ppermute(array, axis, pairs)


VMEM = pl.BlockSpec(memory_space=pltpu.VMEM)
SMEM = pl.BlockSpec(memory_space=pltpu.SMEM)


def per_device(disp, vel, bonds):
    f32 = jnp.float32
    parity = jnp.stack([lax.axis_index("gx") % 2, lax.axis_index("gy") % 2]).astype(jnp.int32)
    edge, block = pl.pallas_call(
        pack_kernel,
        out_shape=(
            jax.ShapeDtypeStruct((8 * FIELDS, LANES), f32),
            jax.ShapeDtypeStruct((FIELDS * BLOCK, LANES), f32),
        ),
        in_specs=[VMEM] * 3,
        out_specs=(VMEM, VMEM),
        name="pack",
    )(disp, vel, bonds)
    odd_edge = swap(edge, "gy", 1)
    even_edge = swap(edge, "gy", 0)
    ends = jax.ShapeDtypeStruct((FIELDS * PITCH, LANES), f32)
    block, first, last = pl.pallas_call(
        halo_kernel,
        out_shape=(jax.ShapeDtypeStruct((FIELDS * BLOCK, LANES), f32), ends, ends),
        in_specs=[SMEM] + [VMEM] * 3,
        out_specs=(VMEM,) * 3,
        name="halo",
    )(parity, block, even_edge, odd_edge)
    odd_block = swap(block, "gx", 1)
    even_block = swap(block, "gx", 0)
    below = shift(last, "gx", 2)
    above = shift(first, "gx", -2)
    out = jax.ShapeDtypeStruct(disp.shape, f32)
    return pl.pallas_call(
        step_kernel,
        out_shape=(out, out),
        in_specs=[SMEM] + [VMEM] * 5,
        out_specs=(VMEM, VMEM),
        scratch_shapes=[
            pltpu.VMEM((FIELDS, LINES, LANES), f32),
            pltpu.VMEM((24, LINES, LANES), f32),
            pltpu.VMEM((14, LINES, LANES), f32),
            pltpu.VMEM((8, LINES, LANES), f32),
        ],
        compiler_params=pltpu.CompilerParams(vmem_limit_bytes=16 * 2**20),
        name="steps",
    )(parity, block, even_block, odd_block, below, above)


def solution(mesh):
    spec = P(None, "gx", "gy")
    return jax.shard_map(
        per_device,
        mesh=mesh,
        in_specs=(spec, spec, spec),
        out_specs=(spec, spec),
        check_vma=False,
    )
```

```python
import math

import jax
import jax.numpy as jnp
from jax import lax
from jax.experimental import pallas as pl
from jax.experimental.pallas import tpu as pltpu
from jax.sharding import PartitionSpec as P

STIFFNESS = 40.0
TIME_STEP = 0.05
SOFTENING = 0.0625
PACK_SHIFT = (0, 3, 10, 17)
LANES = 128

ROWS = 8
PITCH = 9
BLOCK = ROWS * PITCH
FIELDS = 5
HALO = 9
GUARD = 8
LINES = 256


def row_line(row):
    return GUARD + PITCH * (row + HALO)


def lane_ids():
    return lax.broadcasted_iota(jnp.int32, (8, LANES), 1)


def edge_kernel(disp_hbm, vel_hbm, bonds_hbm, edge_ref, disp, vel, bonds, sems):
    copies = []
    for side in range(2):
        cols = pl.ds(side * (ROWS - 1) * LANES, LANES)
        for k, (source, target) in enumerate(
            ((disp_hbm, disp), (vel_hbm, vel), (bonds_hbm, bonds))
        ):
            copies.append(
                pltpu.make_async_copy(source.at[:, :, cols], target.at[side], sems.at[side, k])
            )
    for copy in copies:
        copy.start()
    for copy in copies:
        copy.wait()
    low_half = lane_ids() < LANES // 2
    for part in range(2):
        edge_ref[pl.ds(8 * part, 8), :] = jnp.where(low_half, disp[0, part], disp[1, part])
        edge_ref[pl.ds(8 * part + 16, 8), :] = jnp.where(low_half, vel[0, part], vel[1, part])
    words = [jnp.where(low_half, bonds[0, word], bonds[1, word]) for word in range(4)]
    edge_ref[pl.ds(32, 8), :] = packed(words)


def packed(words):
    total = words[0]
    for word in (1, 2, 3):
        total = total + words[word] * (1 << PACK_SHIFT[word])
    return total.astype(jnp.float32)


def block_kernel(disp_ref, vel_ref, bonds_ref, even_ref, odd_ref, block_ref, first_ref, last_ref):
    low_half = lane_ids() < LANES // 2
    is_even = lax.rem(lax.axis_index("gy"), 2) == 0
    for field in range(FIELDS):
        even = even_ref[pl.ds(8 * field, 8), :]
        odd = odd_ref[pl.ds(8 * field, 8), :]
        from_right = jnp.where(is_even, even, odd)
        from_left = jnp.where(is_even, odd, even)
        lines = [jnp.where(low_half, from_right, from_left)]
        for tile in range(ROWS):
            cols = pl.ds(tile * LANES, LANES)
            if field < 2:
                lines.append(disp_ref[field, :, cols])
            elif field < 4:
                lines.append(vel_ref[field - 2, :, cols])
            else:
                lines.append(packed([bonds_ref[word, :, cols] for word in range(4)]))
        for k, value in enumerate(lines):
            block_ref[pl.ds(field * BLOCK + k, ROWS, stride=PITCH), :] = value
            first_ref[pl.ds(PITCH * field + k, 1), :] = value[:1]
            last_ref[pl.ds(PITCH * field + k, 1), :] = value[7:]


def shifted(here, after, before, by, lanes):
    if by > 0:
        return pltpu.roll(jnp.where(lanes < by, after, here), LANES - by, 1)
    if by < 0:
        return pltpu.roll(jnp.where(lanes >= LANES + by, before, here), -by, 1)
    return here


def force_lines(data, masks, push, pull, start, count, fresh_masks):
    lanes = lane_ids()

    def body(step, carry):
        line = start + 8 * step

        def at(field, offset):
            return data[field, pl.ds(line + offset, 8), :]

        here = [at(f, 0) for f in range(4)]
        after = [at(f, 1) for f in range(4)]
        before = [at(f, -1) for f in range(4)]
        near = []
        words = []
        for row_off in range(4):
            if row_off == 0:
                near.append(here)
            else:
                value = [at(f, -PITCH * row_off) for f in range(4)]
                value[0] = value[0] - float(row_off)
                near.append(value)
            if fresh_masks:
                words.append(at(4, -PITCH * row_off).astype(jnp.int32))
        own = [None] * 4
        for col_off in range(-3, 4):
            far = [shifted(here[f], after[f], before[f], col_off, lanes) for f in range(4)]
            if col_off:
                far[1] = far[1] + float(col_off)
            sum_x = sum_y = None
            for row_off in range(4):
                if row_off == 0 and col_off <= 0:
                    continue
                bit = col_off - 1 if row_off == 0 else col_off + 3
                slot = PACK_SHIFT[row_off] + bit
                squared = row_off * row_off + col_off * col_off
                rest = math.sqrt(squared + SOFTENING)
                base = near[row_off]
                along_x = far[0] - base[0]
                along_y = far[1] - base[1]
                rate_x = far[2] - base[2]
                rate_y = far[3] - base[3]
                inverse = lax.rsqrt(along_x * along_x + (along_y * along_y + SOFTENING))
                dot = along_x * rate_x + along_y * rate_y
                if fresh_masks:
                    mask = jnp.where((words[row_off] & (1 << slot)) != 0, 1.0 / squared, 0.0)
                    masks[slot, pl.ds(line, 8), :] = mask
                else:
                    mask = masks[slot, pl.ds(line, 8), :]
                scale = mask * (
                    STIFFNESS - (STIFFNESS * rest - dot * inverse) * inverse
                )
                pull_x = scale * along_x
                pull_y = scale * along_y
                sum_x = pull_x if sum_x is None else sum_x + pull_x
                sum_y = pull_y if sum_y is None else sum_y + pull_y
                if own[row_off] is None:
                    own[row_off] = (pull_x, pull_y)
                else:
                    own[row_off] = (own[row_off][0] + pull_x, own[row_off][1] + pull_y)
            push[2 * (col_off + 3), pl.ds(line, 8), :] = sum_x
            push[2 * (col_off + 3) + 1, pl.ds(line, 8), :] = sum_y
        for row_off in range(4):
            pull[2 * row_off, pl.ds(line, 8), :] = own[row_off][0]
            pull[2 * row_off + 1, pl.ds(line, 8), :] = own[row_off][1]
        return carry

    lax.fori_loop(0, count, body, 0)


def update_lines(data, push, pull, start, count, which, unroll):
    lanes = lane_ids()

    def change(line, part):
        force = pull[part, pl.ds(line, 8), :]
        for row_off in (1, 2, 3):
            force = force + pull[2 * row_off + part, pl.ds(line + PITCH * row_off, 8), :]
        for col_off in range(-3, 4):
            slot = 2 * (col_off + 3) + part
            here = push[slot, pl.ds(line, 8), :]
            if col_off > 0:
                here = shifted(here, None, push[slot, pl.ds(line - 1, 8), :], -col_off, lanes)
            elif col_off < 0:
                here = shifted(here, push[slot, pl.ds(line + 1, 8), :], None, -col_off, lanes)
            force = force - here
        return (0.5 * TIME_STEP) * force

    def body(step, carry):
        base = start + 8 * unroll * step
        stores = []
        for line in [base + 8 * k for k in range(unroll)]:
            for part in range(2):
                gain = change(line, part)
                speed = data[2 + part, pl.ds(line, 8), :] + gain
                if which == 1:
                    speed = speed + gain
                stores.append((2 + part, line, speed))
                if which < 2:
                    moved = data[part, pl.ds(line, 8), :] + TIME_STEP * speed
                    stores.append((part, line, moved))
        for field, line, value in stores:
            data[field, pl.ds(line, 8), :] = value
        return carry

    lax.fori_loop(0, -(-count // unroll), body, 0)


def step_kernel(
    block_ref, even_ref, odd_ref, below_ref, above_ref,
    disp_ref, vel_ref, data, masks, push, pull,
):
    lanes = lane_ids()
    low_half = lanes < LANES // 2
    is_even = lax.rem(lax.axis_index("gx"), 2) == 0
    even_line = jnp.where(is_even, row_line(8), row_line(-8))
    odd_line = jnp.where(is_even, row_line(-8), row_line(8))
    for field in range(FIELDS):
        for part in range(PITCH):
            source = pl.ds(field * BLOCK + 8 * part, 8)
            data[field, pl.ds(row_line(0) + 8 * part, 8), :] = block_ref[source, :]
            data[field, pl.ds(even_line + 8 * part, 8), :] = even_ref[source, :]
            data[field, pl.ds(odd_line + 8 * part, 8), :] = odd_ref[source, :]
        ends = pl.ds(PITCH * field, PITCH)
        data[field, pl.ds(row_line(-9), PITCH), :] = below_ref[ends, :]
        data[field, pl.ds(row_line(16), PITCH), :] = above_ref[ends, :]
    for field in range(FIELDS):
        lines = [
            (row_line(-8) + 8 * PITCH * k, 8 if k < 3 else 2) for k in range(4)
        ]
        joined = []
        for line, size in lines:
            own = data[field, pl.ds(line, size, stride=PITCH), :]
            ahead = data[field, pl.ds(line - PITCH, size, stride=PITCH), :]
            joined.append(jnp.where(low_half[:size], ahead, own))
        for (line, size), value in zip(lines, joined):
            data[field, pl.ds(line, size, stride=PITCH), :] = value
    for which in range(3):
        reach = 3 * (2 - which)
        low, high = -reach, ROWS + reach
        first, last = row_line(low), row_line(high + 3) + 1
        force_lines(data, masks, push, pull, first, -(-(last - first) // 8), which == 0)
        last = row_line(high) + 1
        update_lines(data, push, pull, first, -(-(last - first) // 8), which, (4, 4, 3)[which])
    for tile in range(ROWS):
        lines = pl.ds(row_line(0) + 1 + tile, ROWS, stride=PITCH)
        cols = pl.ds(tile * LANES, LANES)
        for part in range(2):
            disp_ref[part, :, cols] = data[part, lines, :]
            vel_ref[part, :, cols] = data[2 + part, lines, :]


def shift(array, axis, by):
    count = lax.axis_size(axis)
    return lax.ppermute(array, axis, [(i, (i + by) % count) for i in range(count)])


def swap(array, axis, odd):
    count = lax.axis_size(axis)
    pairs = []
    for i in range(odd, count + odd, 2):
        pairs += [(i % count, (i + 1) % count), ((i + 1) % count, i % count)]
    return lax.ppermute(array, axis, pairs)


VMEM = pl.BlockSpec(memory_space=pltpu.VMEM)


def per_device(disp, vel, bonds):
    f32 = jnp.float32
    small = pltpu.CompilerParams(vmem_limit_bytes=4 * 2**20)
    edge = pl.pallas_call(
        edge_kernel,
        out_shape=jax.ShapeDtypeStruct((8 * FIELDS, LANES), f32),
        in_specs=[pl.BlockSpec(memory_space=pltpu.HBM)] * 3,
        out_specs=VMEM,
        scratch_shapes=[
            pltpu.VMEM((2, 2, ROWS, LANES), f32),
            pltpu.VMEM((2, 2, ROWS, LANES), f32),
            pltpu.VMEM((2, 4, ROWS, LANES), jnp.int32),
            pltpu.SemaphoreType.DMA((2, 3)),
        ],
        compiler_params=small,
        name="edge",
    )(*(pltpu.with_memory_space_constraint(x, pltpu.HBM) for x in (disp, vel, bonds)))
    odd_edge = swap(edge, "gy", 1)
    even_edge = swap(edge, "gy", 0)
    ends = jax.ShapeDtypeStruct((FIELDS * PITCH, LANES), f32)
    block, first, last = pl.pallas_call(
        block_kernel,
        out_shape=(jax.ShapeDtypeStruct((FIELDS * BLOCK, LANES), f32), ends, ends),
        in_specs=[VMEM] * 5,
        out_specs=(VMEM,) * 3,
        compiler_params=small,
        name="block",
    )(disp, vel, bonds, even_edge, odd_edge)
    odd_block = swap(block, "gx", 1)
    even_block = swap(block, "gx", 0)
    below = shift(last, "gx", 2)
    above = shift(first, "gx", -2)
    out = jax.ShapeDtypeStruct(disp.shape, f32)
    return pl.pallas_call(
        step_kernel,
        out_shape=(out, out),
        in_specs=[VMEM] * 5,
        out_specs=(VMEM, VMEM),
        scratch_shapes=[
            pltpu.VMEM((FIELDS, LINES, LANES), f32),
            pltpu.VMEM((24, LINES, LANES), f32),
            pltpu.VMEM((14, LINES, LANES), f32),
            pltpu.VMEM((8, LINES, LANES), f32),
        ],
        compiler_params=pltpu.CompilerParams(vmem_limit_bytes=16 * 2**20),
        name="steps",
    )(block, even_block, odd_block, below, above)


def solution(mesh):
    spec = P(None, "gx", "gy")
    return jax.shard_map(
        per_device,
        mesh=mesh,
        in_specs=(spec, spec, spec),
        out_specs=(spec, spec),
        check_vma=False,
    )
```

```python
import math

import jax
import jax.numpy as jnp
from jax import lax
from jax.experimental import pallas as pl
from jax.experimental.pallas import tpu as pltpu
from jax.sharding import PartitionSpec as P

STIFFNESS = 40.0
TIME_STEP = 0.05
SOFTENING = 0.0625
PACK_SHIFT = (0, 3, 10, 17)
LANES = 128

ROWS = 8
PITCH = 9
BLOCK = ROWS * PITCH
FIELDS = 5
HALO = 9
GUARD = 8
LINES = 256


def row_line(row):
    return GUARD + PITCH * (row + HALO)


def lane_ids():
    return lax.broadcasted_iota(jnp.int32, (8, LANES), 1)


def edge_kernel(disp_hbm, vel_hbm, bonds_hbm, edge_ref, disp, vel, bonds, sems):
    copies = [
        pltpu.make_async_copy(source, target, sems.at[k])
        for k, (source, target) in enumerate(
            ((disp_hbm, disp), (vel_hbm, vel), (bonds_hbm, bonds))
        )
    ]
    for copy in copies:
        copy.start()
    for copy in copies:
        copy.wait()
    low_half = lane_ids() < LANES // 2
    left = pl.ds(0, LANES)
    right = pl.ds((ROWS - 1) * LANES, LANES)

    def ends(ref, part):
        return jnp.where(low_half, ref[part, :, left], ref[part, :, right])

    for part in range(2):
        edge_ref[pl.ds(8 * part, 8), :] = ends(disp, part)
        edge_ref[pl.ds(8 * part + 16, 8), :] = ends(vel, part)
    edge_ref[pl.ds(32, 8), :] = packed([ends(bonds, word) for word in range(4)])


def packed(words):
    total = words[0]
    for word in (1, 2, 3):
        total = total + words[word] * (1 << PACK_SHIFT[word])
    return total.astype(jnp.float32)


def block_kernel(disp_ref, vel_ref, bonds_ref, even_ref, odd_ref, block_ref, first_ref, last_ref):
    low_half = lane_ids() < LANES // 2
    is_even = lax.rem(lax.axis_index("gy"), 2) == 0
    for field in range(FIELDS):
        even = even_ref[pl.ds(8 * field, 8), :]
        odd = odd_ref[pl.ds(8 * field, 8), :]
        from_right = jnp.where(is_even, even, odd)
        from_left = jnp.where(is_even, odd, even)
        lines = [jnp.where(low_half, from_right, from_left)]
        for tile in range(ROWS):
            cols = pl.ds(tile * LANES, LANES)
            if field < 2:
                lines.append(disp_ref[field, :, cols])
            elif field < 4:
                lines.append(vel_ref[field - 2, :, cols])
            else:
                lines.append(packed([bonds_ref[word, :, cols] for word in range(4)]))
        for k, value in enumerate(lines):
            block_ref[pl.ds(field * BLOCK + k, ROWS, stride=PITCH), :] = value
            first_ref[pl.ds(PITCH * field + k, 1), :] = value[:1]
            last_ref[pl.ds(PITCH * field + k, 1), :] = value[7:]


def shifted(here, after, before, by, lanes):
    if by > 0:
        return pltpu.roll(jnp.where(lanes < by, after, here), LANES - by, 1)
    if by < 0:
        return pltpu.roll(jnp.where(lanes >= LANES + by, before, here), -by, 1)
    return here


def force_lines(data, masks, push, pull, start, count, fresh_masks):
    lanes = lane_ids()

    def body(step, carry):
        line = start + 8 * step

        def at(field, offset):
            return data[field, pl.ds(line + offset, 8), :]

        here = [at(f, 0) for f in range(4)]
        after = [at(f, 1) for f in range(4)]
        before = [at(f, -1) for f in range(4)]
        near = []
        words = []
        for row_off in range(4):
            if row_off == 0:
                near.append(here)
            else:
                value = [at(f, -PITCH * row_off) for f in range(4)]
                value[0] = value[0] - float(row_off)
                near.append(value)
            if fresh_masks:
                words.append(at(4, -PITCH * row_off).astype(jnp.int32))
        own = [None] * 4
        main = [None] * 2
        carry_over = [None] * 2
        for col_off in range(-3, 4):
            far = [shifted(here[f], after[f], before[f], col_off, lanes) for f in range(4)]
            if col_off:
                far[1] = far[1] + float(col_off)
            sums = [None] * 2
            for row_off in range(4):
                if row_off == 0 and col_off <= 0:
                    continue
                bit = col_off - 1 if row_off == 0 else col_off + 3
                slot = PACK_SHIFT[row_off] + bit
                squared = row_off * row_off + col_off * col_off
                rest = math.sqrt(squared + SOFTENING)
                base = near[row_off]
                along_x = far[0] - base[0]
                along_y = far[1] - base[1]
                rate_x = far[2] - base[2]
                rate_y = far[3] - base[3]
                inverse = lax.rsqrt(along_x * along_x + (along_y * along_y + SOFTENING))
                dot = along_x * rate_x + along_y * rate_y
                if fresh_masks:
                    mask = jnp.where((words[row_off] & (1 << slot)) != 0, 1.0 / squared, 0.0)
                    masks[slot, pl.ds(line, 8), :] = mask
                else:
                    mask = masks[slot, pl.ds(line, 8), :]
                scale = mask * (STIFFNESS - (STIFFNESS * rest - dot * inverse) * inverse)
                pulled = (scale * along_x, scale * along_y)
                sums = [added(sums[part], pulled[part]) for part in range(2)]
                own[row_off] = [
                    added(own[row_off][part] if own[row_off] else None, pulled[part])
                    for part in range(2)
                ]
            for part in range(2):
                moved = sums[part]
                if col_off:
                    moved = pltpu.roll(moved, col_off % LANES, 1)
                    wrapped = lanes < col_off if col_off > 0 else lanes >= LANES + col_off
                    carry_over[part] = added(carry_over[part], jnp.where(wrapped, moved, 0.0))
                main[part] = added(main[part], moved)
        for part in range(2):
            push[part, pl.ds(line, 8), :] = main[part] - carry_over[part]
            push[2 + part, pl.ds(line, 8), :] = carry_over[part]
            for row_off in range(4):
                pull[2 * row_off + part, pl.ds(line, 8), :] = own[row_off][part]
        return carry

    lax.fori_loop(0, count, body, 0)


def added(total, value):
    return value if total is None else total + value


def update_lines(data, push, pull, start, count, which, unroll):
    low_half = lane_ids() < LANES // 2

    def change(line, part):
        force = pull[part, pl.ds(line, 8), :]
        for row_off in (1, 2, 3):
            force = force + pull[2 * row_off + part, pl.ds(line + PITCH * row_off, 8), :]
        carried = jnp.where(
            low_half, push[2 + part, pl.ds(line - 1, 8), :], push[2 + part, pl.ds(line + 1, 8), :]
        )
        return (0.5 * TIME_STEP) * (force - push[part, pl.ds(line, 8), :] - carried)

    def body(step, carry):
        base = start + 8 * unroll * step
        stores = []
        for line in [base + 8 * k for k in range(unroll)]:
            for part in range(2):
                gain = change(line, part)
                speed = data[2 + part, pl.ds(line, 8), :] + gain
                if which == 1:
                    speed = speed + gain
                stores.append((2 + part, line, speed))
                if which < 2:
                    moved = data[part, pl.ds(line, 8), :] + TIME_STEP * speed
                    stores.append((part, line, moved))
        for field, line, value in stores:
            data[field, pl.ds(line, 8), :] = value
        return carry

    lax.fori_loop(0, -(-count // unroll), body, 0)


def first_kernel(block_ref, even_ref, odd_ref, data, masks, push, pull):
    low_half = lane_ids() < LANES // 2
    is_even = lax.rem(lax.axis_index("gx"), 2) == 0
    even_line = jnp.where(is_even, row_line(8), row_line(-8))
    odd_line = jnp.where(is_even, row_line(-8), row_line(8))
    for field in range(FIELDS):
        for part in range(PITCH):
            source = pl.ds(field * BLOCK + 8 * part, 8)
            data[field, pl.ds(row_line(0) + 8 * part, 8), :] = block_ref[source, :]
            data[field, pl.ds(even_line + 8 * part, 8), :] = even_ref[source, :]
            data[field, pl.ds(odd_line + 8 * part, 8), :] = odd_ref[source, :]
    for field in range(FIELDS):
        firsts = [row_line(row) for row in (-8, 0, 8)]
        heads = [data[field, pl.ds(line, 8, stride=PITCH), :] for line in firsts]
        below = [data[field, pl.ds(line - PITCH, 8, stride=PITCH), :] for line in firsts]
        final = data[field, pl.ds(row_line(15), 1), :]
        for line, head, last in zip(firsts, heads, below):
            data[field, pl.ds(line, 8, stride=PITCH), :] = jnp.where(low_half, last, head)
        data[field, pl.ds(row_line(16), 1), :] = final
    first, last = row_line(-5), row_line(16)
    force_lines(data, masks, push, pull, first, -(-(last - first) // 8), True)


def rest_kernel(
    below_ref, above_ref, data_in, masks_in, push_in, pull_in,
    disp_ref, vel_ref, data, masks, push, pull,
):
    low = lax.broadcasted_iota(jnp.int32, (1, LANES), 1) < LANES // 2
    for field in range(FIELDS):
        below = below_ref[pl.ds(PITCH * field, PITCH), :]
        above = above_ref[pl.ds(PITCH * field, PITCH), :]
        data[field, pl.ds(row_line(-9), PITCH), :] = below
        head = pl.ds(row_line(-8), 1)
        data[field, head, :] = jnp.where(low, below[:1], data[field, head, :])
        head = pl.ds(row_line(16), 1)
        kept = data[field, head, :]
        data[field, pl.ds(row_line(16), PITCH), :] = above
        data[field, head, :] = jnp.where(low, kept, above[:1])
        data[field, pl.ds(row_line(17), 1), :] = above[:1]
    force_lines(data, masks, push, pull, row_line(-6), 2, True)
    force_lines(data, masks, push, pull, row_line(16), 2, True)
    for which in range(3):
        reach = 3 * (2 - which)
        low, high = -reach, ROWS + reach
        first, last = row_line(low), row_line(high + 3) + 1
        if which:
            force_lines(data, masks, push, pull, first, -(-(last - first) // 8), False)
        last = row_line(high) + 1
        update_lines(data, push, pull, first, -(-(last - first) // 8), which, (4, 4, 3)[which])
    for tile in range(ROWS):
        lines = pl.ds(row_line(0) + 1 + tile, ROWS, stride=PITCH)
        cols = pl.ds(tile * LANES, LANES)
        for part in range(2):
            disp_ref[part, :, cols] = data[part, lines, :]
            vel_ref[part, :, cols] = data[2 + part, lines, :]


def shift(array, axis, by):
    count = lax.axis_size(axis)
    return lax.ppermute(array, axis, [(i, (i + by) % count) for i in range(count)])


def swap(array, axis, odd):
    count = lax.axis_size(axis)
    pairs = []
    for i in range(odd, count + odd, 2):
        pairs += [(i % count, (i + 1) % count), ((i + 1) % count, i % count)]
    return lax.ppermute(array, axis, pairs)


VMEM = pl.BlockSpec(memory_space=pltpu.VMEM)


def per_device(disp, vel, bonds):
    f32 = jnp.float32
    small = pltpu.CompilerParams(vmem_limit_bytes=4 * 2**20)
    edge, disp, vel, bonds = pl.pallas_call(
        edge_kernel,
        out_shape=(
            jax.ShapeDtypeStruct((8 * FIELDS, LANES), f32),
            jax.ShapeDtypeStruct(disp.shape, disp.dtype),
            jax.ShapeDtypeStruct(vel.shape, vel.dtype),
            jax.ShapeDtypeStruct(bonds.shape, bonds.dtype),
        ),
        in_specs=[pl.BlockSpec(memory_space=pltpu.HBM)] * 3,
        out_specs=(VMEM,) * 4,
        scratch_shapes=[pltpu.SemaphoreType.DMA((3,))],
        compiler_params=small,
        name="edge",
    )(*(pltpu.with_memory_space_constraint(x, pltpu.HBM) for x in (disp, vel, bonds)))
    odd_edge = swap(edge, "gy", 1)
    even_edge = swap(edge, "gy", 0)
    ends = jax.ShapeDtypeStruct((FIELDS * PITCH, LANES), f32)
    block, first, last = pl.pallas_call(
        block_kernel,
        out_shape=(jax.ShapeDtypeStruct((FIELDS * BLOCK, LANES), f32), ends, ends),
        in_specs=[VMEM] * 5,
        out_specs=(VMEM,) * 3,
        compiler_params=small,
        name="block",
    )(disp, vel, bonds, even_edge, odd_edge)
    odd_block = swap(block, "gx", 1)
    even_block = swap(block, "gx", 0)
    below = shift(last, "gx", 2)
    above = shift(first, "gx", -2)
    work = tuple(
        jax.ShapeDtypeStruct((count, LINES, LANES), f32) for count in (FIELDS, 24, 4, 8)
    )
    state = pl.pallas_call(
        first_kernel,
        out_shape=work,
        in_specs=[VMEM] * 3,
        out_specs=(VMEM,) * 4,
        compiler_params=small,
        cost_estimate=pl.CostEstimate(
            flops=20_000_000, bytes_accessed=8_000_000, transcendentals=500_000
        ),
        name="first",
    )(block, even_block, odd_block)
    out = jax.ShapeDtypeStruct(disp.shape, f32)
    results = pl.pallas_call(
        rest_kernel,
        out_shape=(out, out) + work,
        in_specs=[VMEM] * 6,
        out_specs=(VMEM,) * 6,
        input_output_aliases={2: 2, 3: 3, 4: 4, 5: 5},
        compiler_params=small,
        name="rest",
    )(below, above, *state)
    return results[0], results[1]


def solution(mesh):
    spec = P(None, "gx", "gy")
    return jax.shard_map(
        per_device,
        mesh=mesh,
        in_specs=(spec, spec, spec),
        out_specs=(spec, spec),
        check_vma=False,
    )
```

```python
import math

import jax
import jax.numpy as jnp
from jax import lax
from jax.experimental import pallas as pl
from jax.experimental.pallas import tpu as pltpu
from jax.sharding import PartitionSpec as P

STIFFNESS = 40.0
TIME_STEP = 0.05
SOFTENING = 0.0625
PACK_SHIFT = (0, 3, 10, 17)
LANES = 128

ROWS = 8
PITCH = 9
BLOCK = ROWS * PITCH
FIELDS = 5
HALO = 9
GUARD = 8
LINES = 256


def row_line(row):
    return GUARD + PITCH * (row + HALO)


def lane_ids():
    return lax.broadcasted_iota(jnp.int32, (8, LANES), 1)


def edge_kernel(disp_hbm, vel_hbm, bonds_hbm, edge_ref, disp, vel, bonds, sems):
    copies = [
        pltpu.make_async_copy(source, target, sems.at[k])
        for k, (source, target) in enumerate(
            ((disp_hbm, disp), (vel_hbm, vel), (bonds_hbm, bonds))
        )
    ]
    for copy in copies:
        copy.start()
    for copy in copies:
        copy.wait()
    low_half = lane_ids() < LANES // 2
    left = pl.ds(0, LANES)
    right = pl.ds((ROWS - 1) * LANES, LANES)

    def ends(ref, part):
        return jnp.where(low_half, ref[part, :, left], ref[part, :, right])

    for part in range(2):
        edge_ref[pl.ds(8 * part, 8), :] = ends(disp, part)
        edge_ref[pl.ds(8 * part + 16, 8), :] = ends(vel, part)
    edge_ref[pl.ds(32, 8), :] = packed([ends(bonds, word) for word in range(4)])


def packed(words):
    total = words[0]
    for word in (1, 2, 3):
        total = total + words[word] * (1 << PACK_SHIFT[word])
    return total.astype(jnp.float32)


def block_kernel(disp_ref, vel_ref, bonds_ref, even_ref, odd_ref, block_ref, first_ref, last_ref):
    low_half = lane_ids() < LANES // 2
    is_even = lax.rem(lax.axis_index("gy"), 2) == 0
    for field in range(FIELDS):
        even = even_ref[pl.ds(8 * field, 8), :]
        odd = odd_ref[pl.ds(8 * field, 8), :]
        from_right = jnp.where(is_even, even, odd)
        from_left = jnp.where(is_even, odd, even)
        lines = [jnp.where(low_half, from_right, from_left)]
        for tile in range(ROWS):
            cols = pl.ds(tile * LANES, LANES)
            if field < 2:
                lines.append(disp_ref[field, :, cols])
            elif field < 4:
                lines.append(vel_ref[field - 2, :, cols])
            else:
                lines.append(packed([bonds_ref[word, :, cols] for word in range(4)]))
        for k, value in enumerate(lines):
            block_ref[pl.ds(field * BLOCK + k, ROWS, stride=PITCH), :] = value
            first_ref[pl.ds(PITCH * field + k, 1), :] = value[:1]
            last_ref[pl.ds(PITCH * field + k, 1), :] = value[7:]


def look_ahead(data, words, ahead, ahead_words, line, lanes, with_words):
    found = []
    here = [data[f, pl.ds(line, 8), :] for f in range(4)]
    after = [data[f, pl.ds(line + 1, 8), :] for f in range(4)]
    for by in (1, 2, 3):
        far = []
        for f in range(4):
            value = pltpu.roll(jnp.where(lanes < by, after[f], here[f]), LANES - by, 1)
            if f == 1:
                value = value + float(by)
            ahead[4 * (by - 1) + f, pl.ds(line, 8), :] = value
            far.append(value)
        found.append(far)
        if with_words:
            ahead_words[by - 1, pl.ds(line, 8), :] = pltpu.roll(
                jnp.where(lanes < by, words[pl.ds(line + 1, 8), :], words[pl.ds(line, 8), :]),
                LANES - by,
                1,
            )
    return here, found


def prepare_lines(data, words, ahead, ahead_words, start, count, with_words):
    lanes = lane_ids()
    for step in range(count):
        look_ahead(data, words, ahead, ahead_words, start + 8 * step, lanes, with_words)


def bond_pull(far, near, row_off, col_off, mask):
    rest = math.sqrt(row_off * row_off + col_off * col_off + SOFTENING)
    along_x = far[0] - near[0]
    along_y = far[1] - near[1]
    rate_x = far[2] - near[2]
    rate_y = far[3] - near[3]
    inverse = lax.rsqrt(along_x * along_x + (along_y * along_y + SOFTENING))
    dot = along_x * rate_x + along_y * rate_y
    scale = mask * (STIFFNESS - (STIFFNESS * rest - dot * inverse) * inverse)
    return (scale * along_x, scale * along_y)


def added(total, value):
    if total is None:
        return list(value)
    return [total[part] + value[part] for part in range(2)]


def force_lines(state, start, count, fresh_masks):
    data, words, ahead, ahead_words, masks, pull, push = state
    lanes = lane_ids()

    def body(step, carry):
        line = start + 8 * step
        here, found = look_ahead(data, words, ahead, ahead_words, line, lanes, fresh_masks)

        def at(ref, k, offset):
            return ref[k, pl.ds(line - PITCH * offset, 8), :]

        def mask_of(slot, row_off, col_off, word):
            if not fresh_masks:
                return masks[slot, pl.ds(line, 8), :]
            weight = 1.0 / (row_off * row_off + col_off * col_off)
            mask = jnp.where((word & (1 << slot)) != 0, weight, 0.0)
            masks[slot, pl.ds(line, 8), :] = mask
            return mask

        def store(ref, k, value):
            for part in range(2):
                ref[2 * k + part, pl.ds(line, 8), :] = value[part]

        own = [None] * 4
        reach = [None] * 4
        for row_off in range(4):
            near = here if row_off == 0 else [at(data, f, row_off) for f in range(4)]
            if row_off:
                near[0] = near[0] - float(row_off)
            word = words[pl.ds(line - PITCH * row_off, 8), :] if fresh_masks else None
            for col_off in range(4):
                if row_off == 0 and col_off == 0:
                    continue
                far = found[col_off - 1] if col_off else here
                slot = col_off - 1 if row_off == 0 else PACK_SHIFT[row_off] + col_off + 3
                mask = mask_of(slot, row_off, col_off, word)
                value = bond_pull(far, near, row_off, col_off, mask)
                own[row_off] = added(own[row_off], value)
                reach[col_off] = added(reach[col_off], value)
        for col_off in range(4):
            store(push, col_off, reach[col_off])
        for row_off in (1, 2, 3):
            near = [here[0] + float(row_off)] + list(here[1:])
            for col_off in (1, 2, 3):
                far = [at(ahead, 4 * (col_off - 1) + f, row_off) for f in range(4)]
                slot = PACK_SHIFT[row_off] - col_off + 3
                word = at(ahead_words, col_off - 1, row_off) if fresh_masks else None
                mask = mask_of(slot, row_off, col_off, word)
                value = bond_pull(far, near, row_off, col_off, mask)
                own[0] = added(own[0], value)
                store(push, 3 * row_off + col_off, value)
        for row_off in range(4):
            store(pull, row_off, own[row_off])
        return carry

    lax.fori_loop(0, count, body, 0)


def update_lines(state, over, start, count, which, unroll):
    data, _, _, _, _, pull, push = state
    lanes = lane_ids()

    def force_at(line, part):
        def at(ref, k, offset):
            return ref[2 * k + part, pl.ds(line + PITCH * offset, 8), :]

        force = at(pull, 0, 0) - at(push, 0, 0)
        for row_off in (1, 2, 3):
            force = force + at(pull, row_off, row_off)
        wrapped = None
        for col_off in (1, 2, 3):
            total = at(push, col_off, 0)
            for row_off in (1, 2, 3):
                total = total + at(push, 3 * row_off + col_off, row_off)
            total = pltpu.roll(total, col_off, 1)
            inside = lanes >= col_off
            force = force - jnp.where(inside, total, 0.0)
            outside = jnp.where(inside, 0.0, total)
            wrapped = outside if wrapped is None else wrapped + outside
        over[part, pl.ds(line, 8), :] = wrapped
        return force

    def body(step, carry):
        base = start + 8 * unroll * step
        lines = [base + 8 * k for k in range(unroll)]
        forces = [[force_at(line, part) for part in range(2)] for line in lines]
        stores = []
        for line, both in zip(lines, forces):
            for part in range(2):
                gain = (0.5 * TIME_STEP) * (both[part] - over[part, pl.ds(line - 1, 8), :])
                speed = data[2 + part, pl.ds(line, 8), :] + gain
                if which == 1:
                    speed = speed + gain
                stores.append((2 + part, line, speed))
                if which < 2:
                    moved = data[part, pl.ds(line, 8), :] + TIME_STEP * speed
                    stores.append((part, line, moved))
        for field, line, value in stores:
            data[field, pl.ds(line, 8), :] = value
        return carry

    lax.fori_loop(0, -(-count // unroll), body, 0)


def first_kernel(block_ref, even_ref, odd_ref, *state):
    data, words = state[:2]
    low_half = lane_ids() < LANES // 2
    is_even = lax.rem(lax.axis_index("gx"), 2) == 0
    even_line = jnp.where(is_even, row_line(8), row_line(-8))
    odd_line = jnp.where(is_even, row_line(-8), row_line(8))

    def get(field, lines):
        return data[field, lines, :] if field < 4 else words[lines, :]

    def put(field, lines, value):
        if field < 4:
            data[field, lines, :] = value
        else:
            words[lines, :] = value

    for field in range(FIELDS):
        for part in range(PITCH):
            source = pl.ds(field * BLOCK + 8 * part, 8)
            for ref, line in (
                (block_ref, row_line(0)), (even_ref, even_line), (odd_ref, odd_line)
            ):
                value = ref[source, :]
                if field == 4:
                    value = value.astype(jnp.int32)
                put(field, pl.ds(line + 8 * part, 8), value)
    for field in range(FIELDS):
        firsts = [row_line(row) for row in (-8, 0, 8)]
        heads = [get(field, pl.ds(line, 8, stride=PITCH)) for line in firsts]
        below = [get(field, pl.ds(line - PITCH, 8, stride=PITCH)) for line in firsts]
        final = get(field, pl.ds(row_line(15), 1))
        for line, head, last in zip(firsts, heads, below):
            put(field, pl.ds(line, 8, stride=PITCH), jnp.where(low_half, last, head))
        put(field, pl.ds(row_line(16), 1), final)
    first, last = row_line(-5), row_line(16)
    prepare_lines(*state[:4], row_line(-8), 4, True)
    force_lines(state, first, -(-(last - first) // 8), True)


def rest_kernel(below_ref, above_ref, *refs):
    count = len(refs) - 3
    state_count = count // 2
    disp_ref, vel_ref = refs[state_count : state_count + 2]
    state = refs[state_count + 2 : -1]
    over = refs[-1]
    data, words = state[:2]
    low = lax.broadcasted_iota(jnp.int32, (1, LANES), 1) < LANES // 2
    for field in range(FIELDS):
        below = below_ref[pl.ds(PITCH * field, PITCH), :]
        above = above_ref[pl.ds(PITCH * field, PITCH), :]
        if field == 4:
            below, above = below.astype(jnp.int32), above.astype(jnp.int32)
        target = data.at[field] if field < 4 else words
        target[pl.ds(row_line(-9), PITCH), :] = below
        head = pl.ds(row_line(-8), 1)
        target[head, :] = jnp.where(low, below[:1], target[head, :])
        head = pl.ds(row_line(16), 1)
        kept = target[head, :]
        target[pl.ds(row_line(16), PITCH), :] = above
        target[head, :] = jnp.where(low, kept, above[:1])
        target[pl.ds(row_line(17), 1), :] = above[:1]
    prepare_lines(*state[:4], row_line(-9), 4, True)
    force_lines(state, row_line(-6), 2, True)
    force_lines(state, row_line(16), 2, True)
    for which in range(3):
        reach = 3 * (2 - which)
        low_row, high_row = -reach, ROWS + reach
        first, last = row_line(low_row), row_line(high_row + 3) + 1
        if which:
            prepare_lines(*state[:4], row_line(low_row - 3), 4, False)
            force_lines(state, first, -(-(last - first) // 8), False)
        last = row_line(high_row) + 1
        update_lines(state, over, first, -(-(last - first) // 8), which, (4, 4, 3)[which])
    for tile in range(ROWS):
        lines = pl.ds(row_line(0) + 1 + tile, ROWS, stride=PITCH)
        cols = pl.ds(tile * LANES, LANES)
        for part in range(2):
            disp_ref[part, :, cols] = data[part, lines, :]
            vel_ref[part, :, cols] = data[2 + part, lines, :]


def shift(array, axis, by):
    count = lax.axis_size(axis)
    return lax.ppermute(array, axis, [(i, (i + by) % count) for i in range(count)])


def swap(array, axis, odd):
    count = lax.axis_size(axis)
    pairs = []
    for i in range(odd, count + odd, 2):
        pairs += [(i % count, (i + 1) % count), ((i + 1) % count, i % count)]
    return lax.ppermute(array, axis, pairs)


VMEM = pl.BlockSpec(memory_space=pltpu.VMEM)


def per_device(disp, vel, bonds):
    f32 = jnp.float32
    small = pltpu.CompilerParams(vmem_limit_bytes=4 * 2**20)
    edge, disp, vel, bonds = pl.pallas_call(
        edge_kernel,
        out_shape=(
            jax.ShapeDtypeStruct((8 * FIELDS, LANES), f32),
            jax.ShapeDtypeStruct(disp.shape, disp.dtype),
            jax.ShapeDtypeStruct(vel.shape, vel.dtype),
            jax.ShapeDtypeStruct(bonds.shape, bonds.dtype),
        ),
        in_specs=[pl.BlockSpec(memory_space=pltpu.HBM)] * 3,
        out_specs=(VMEM,) * 4,
        scratch_shapes=[pltpu.SemaphoreType.DMA((3,))],
        compiler_params=small,
        name="edge",
    )(*(pltpu.with_memory_space_constraint(x, pltpu.HBM) for x in (disp, vel, bonds)))
    odd_edge = swap(edge, "gy", 1)
    even_edge = swap(edge, "gy", 0)
    ends = jax.ShapeDtypeStruct((FIELDS * PITCH, LANES), f32)
    block, first, last = pl.pallas_call(
        block_kernel,
        out_shape=(jax.ShapeDtypeStruct((FIELDS * BLOCK, LANES), f32), ends, ends),
        in_specs=[VMEM] * 5,
        out_specs=(VMEM,) * 3,
        compiler_params=small,
        name="block",
    )(disp, vel, bonds, even_edge, odd_edge)
    odd_block = swap(block, "gx", 1)
    even_block = swap(block, "gx", 0)
    below = shift(last, "gx", 2)
    above = shift(first, "gx", -2)
    work = (
        jax.ShapeDtypeStruct((4, LINES, LANES), f32),
        jax.ShapeDtypeStruct((LINES, LANES), jnp.int32),
        jax.ShapeDtypeStruct((12, LINES, LANES), f32),
        jax.ShapeDtypeStruct((3, LINES, LANES), jnp.int32),
        jax.ShapeDtypeStruct((24, LINES, LANES), f32),
        jax.ShapeDtypeStruct((8, LINES, LANES), f32),
        jax.ShapeDtypeStruct((26, LINES, LANES), f32),
    )
    state = pl.pallas_call(
        first_kernel,
        out_shape=work,
        in_specs=[VMEM] * 3,
        out_specs=(VMEM,) * len(work),
        compiler_params=small,
        cost_estimate=pl.CostEstimate(
            flops=20_000_000, bytes_accessed=8_000_000, transcendentals=500_000
        ),
        name="first",
    )(block, even_block, odd_block)
    out = jax.ShapeDtypeStruct(disp.shape, f32)
    results = pl.pallas_call(
        rest_kernel,
        out_shape=(out, out) + work,
        in_specs=[VMEM] * (2 + len(work)),
        out_specs=(VMEM,) * (2 + len(work)),
        scratch_shapes=[pltpu.VMEM((2, LINES, LANES), f32)],
        input_output_aliases={2 + k: 2 + k for k in range(len(work))},
        compiler_params=small,
        name="rest",
    )(below, above, *state)
    return results[0], results[1]


def solution(mesh):
    spec = P(None, "gx", "gy")
    return jax.shard_map(
        per_device,
        mesh=mesh,
        in_specs=(spec, spec, spec),
        out_specs=(spec, spec),
        check_vma=False,
    )
```

```python
import math

import jax
import jax.numpy as jnp
from jax import lax
from jax.experimental import pallas as pl
from jax.experimental.pallas import tpu as pltpu
from jax.sharding import PartitionSpec as P

STIFFNESS = 40.0
TIME_STEP = 0.05
SOFTENING = 0.0625
PACK_SHIFT = (0, 3, 10, 17)
LANES = 128

ROWS = 8
PITCH = 9
BLOCK = ROWS * PITCH
FIELDS = 5
HALO = 9
GUARD = 8
LINES = 272


def row_line(row):
    return GUARD + PITCH * (row + HALO)


def lane_ids():
    return lax.broadcasted_iota(jnp.int32, (8, LANES), 1)


def edge_kernel(disp_hbm, vel_hbm, bonds_hbm, edge_ref, disp, vel, bonds, sems):
    copies = [
        pltpu.make_async_copy(source, target, sems.at[k])
        for k, (source, target) in enumerate(
            ((disp_hbm, disp), (vel_hbm, vel), (bonds_hbm, bonds))
        )
    ]
    for copy in copies:
        copy.start()
    for copy in copies:
        copy.wait()
    low_half = lane_ids() < LANES // 2
    left = pl.ds(0, LANES)
    right = pl.ds((ROWS - 1) * LANES, LANES)

    def ends(ref, part):
        return jnp.where(low_half, ref[part, :, left], ref[part, :, right])

    for part in range(2):
        edge_ref[pl.ds(8 * part, 8), :] = ends(disp, part)
        edge_ref[pl.ds(8 * part + 16, 8), :] = ends(vel, part)
    edge_ref[pl.ds(32, 8), :] = packed([ends(bonds, word) for word in range(4)])


def packed(words):
    total = words[0]
    for word in (1, 2, 3):
        total = total + words[word] * (1 << PACK_SHIFT[word])
    return total.astype(jnp.float32)


def block_kernel(disp_ref, vel_ref, bonds_ref, even_ref, odd_ref, block_ref, first_ref, last_ref):
    low_half = lane_ids() < LANES // 2
    is_even = lax.rem(lax.axis_index("gy"), 2) == 0
    for field in range(FIELDS):
        even = even_ref[pl.ds(8 * field, 8), :]
        odd = odd_ref[pl.ds(8 * field, 8), :]
        from_right = jnp.where(is_even, even, odd)
        from_left = jnp.where(is_even, odd, even)
        lines = [jnp.where(low_half, from_right, from_left)]
        for tile in range(ROWS):
            cols = pl.ds(tile * LANES, LANES)
            if field < 2:
                lines.append(disp_ref[field, :, cols])
            elif field < 4:
                lines.append(vel_ref[field - 2, :, cols])
            else:
                lines.append(packed([bonds_ref[word, :, cols] for word in range(4)]))
        for k, value in enumerate(lines):
            block_ref[pl.ds(field * BLOCK + k, ROWS, stride=PITCH), :] = value
            first_ref[pl.ds(PITCH * field + k, 1), :] = value[:1]
            last_ref[pl.ds(PITCH * field + k, 1), :] = value[7:]


def look_ahead(data, ahead, line, lanes):
    here = [data[f, pl.ds(line, 8), :] for f in range(4)]
    after = [data[f, pl.ds(line + 1, 8), :] for f in range(4)]
    for by in (1, 2, 3):
        for f in range(4):
            value = pltpu.roll(jnp.where(lanes < by, after[f], here[f]), LANES - by, 1)
            if f == 1:
                value = value + float(by)
            ahead[4 * (by - 1) + f, pl.ds(line, 8), :] = value


def prepare_lines(state, start, count):
    lanes = lane_ids()
    for step in range(count):
        look_ahead(state[0], state[2], start + 8 * step, lanes)


def mask_lines(state, start, count, ahead_start, ahead_count):
    _, words, _, ahead_words, masks, _, _ = state
    lanes = lane_ids()
    for step in range(ahead_count):
        line = ahead_start + 8 * step
        here, after = words[pl.ds(line, 8), :], words[pl.ds(line + 1, 8), :]
        for by in (1, 2, 3):
            ahead_words[by - 1, pl.ds(line, 8), :] = pltpu.roll(
                jnp.where(lanes < by, after, here), LANES - by, 1
            )

    def body(step, carry):
        line = start + 8 * step

        def put(slot, row_off, col_off, word):
            weight = 1.0 / (row_off * row_off + col_off * col_off)
            masks[slot, pl.ds(line, 8), :] = jnp.where((word & (1 << slot)) != 0, weight, 0.0)

        for row_off in range(4):
            word = words[pl.ds(line - PITCH * row_off, 8), :]
            for col_off in range(4):
                if row_off == 0:
                    if col_off:
                        put(col_off - 1, row_off, col_off, word)
                    continue
                put(PACK_SHIFT[row_off] + col_off + 3, row_off, col_off, word)
                if col_off:
                    far_word = ahead_words[col_off - 1, pl.ds(line - PITCH * row_off, 8), :]
                    put(PACK_SHIFT[row_off] - col_off + 3, row_off, col_off, far_word)
        return carry

    lax.fori_loop(0, count, body, 0)


def bond_pull(far, near, row_off, col_off, mask):
    rest = math.sqrt(row_off * row_off + col_off * col_off + SOFTENING)
    along_x = far[0] - near[0]
    along_y = far[1] - near[1]
    rate_x = far[2] - near[2]
    rate_y = far[3] - near[3]
    inverse = lax.rsqrt(along_x * along_x + (along_y * along_y + SOFTENING))
    dot = along_x * rate_x + along_y * rate_y
    scale = mask * (STIFFNESS - (STIFFNESS * rest - dot * inverse) * inverse)
    return (scale * along_x, scale * along_y)


def added(total, value):
    if total is None:
        return list(value)
    return [total[part] + value[part] for part in range(2)]


def force_lines(state, start, count):
    data, _, ahead, _, masks, pull, push = state
    lanes = lane_ids()

    def body(step, carry):
        line = start + 8 * step
        here = [data[f, pl.ds(line, 8), :] for f in range(4)]
        found = [[ahead[4 * b + f, pl.ds(line, 8), :] for f in range(4)] for b in range(3)]
        look_ahead(data, ahead, line + 8, lanes)

        def at(ref, k, offset):
            return ref[k, pl.ds(line - PITCH * offset, 8), :]

        def store(ref, k, value):
            for part in range(2):
                ref[2 * k + part, pl.ds(line, 8), :] = value[part]

        own = [None] * 4
        reach = [None] * 4
        for row_off in range(4):
            near = here if row_off == 0 else [at(data, f, row_off) for f in range(4)]
            if row_off:
                near[0] = near[0] - float(row_off)
            for col_off in range(4):
                if row_off == 0 and col_off == 0:
                    continue
                far = found[col_off - 1] if col_off else here
                slot = col_off - 1 if row_off == 0 else PACK_SHIFT[row_off] + col_off + 3
                mask = masks[slot, pl.ds(line, 8), :]
                value = bond_pull(far, near, row_off, col_off, mask)
                own[row_off] = added(own[row_off], value)
                reach[col_off] = added(reach[col_off], value)
        for col_off in range(4):
            store(push, col_off, reach[col_off])
        for row_off in (1, 2, 3):
            near = [here[0] + float(row_off)] + list(here[1:])
            for col_off in (1, 2, 3):
                far = [at(ahead, 4 * (col_off - 1) + f, row_off) for f in range(4)]
                slot = PACK_SHIFT[row_off] - col_off + 3
                mask = masks[slot, pl.ds(line, 8), :]
                value = bond_pull(far, near, row_off, col_off, mask)
                own[0] = added(own[0], value)
                store(push, 3 * row_off + col_off, value)
        for row_off in range(4):
            store(pull, row_off, own[row_off])
        return carry

    lax.fori_loop(0, count, body, 0)


def update_lines(state, over, start, count, which, unroll):
    data, _, _, _, _, pull, push = state
    lanes = lane_ids()

    def force_at(line, part):
        def at(ref, k, offset):
            return ref[2 * k + part, pl.ds(line + PITCH * offset, 8), :]

        force = at(pull, 0, 0) - at(push, 0, 0)
        for row_off in (1, 2, 3):
            force = force + at(pull, row_off, row_off)
        wrapped = None
        for col_off in (1, 2, 3):
            total = at(push, col_off, 0)
            for row_off in (1, 2, 3):
                total = total + at(push, 3 * row_off + col_off, row_off)
            total = pltpu.roll(total, col_off, 1)
            inside = lanes >= col_off
            force = force - jnp.where(inside, total, 0.0)
            outside = jnp.where(inside, 0.0, total)
            wrapped = outside if wrapped is None else wrapped + outside
        over[part, pl.ds(line, 8), :] = wrapped
        return force

    def body(step, carry):
        base = start + 8 * unroll * step
        lines = [base + 8 * k for k in range(unroll)]
        forces = [[force_at(line, part) for part in range(2)] for line in lines]
        stores = []
        for line, both in zip(lines, forces):
            for part in range(2):
                gain = (0.5 * TIME_STEP) * (both[part] - over[part, pl.ds(line - 1, 8), :])
                speed = data[2 + part, pl.ds(line, 8), :] + gain
                if which == 1:
                    speed = speed + gain
                stores.append((2 + part, line, speed))
                if which < 2:
                    moved = data[part, pl.ds(line, 8), :] + TIME_STEP * speed
                    stores.append((part, line, moved))
        for field, line, value in stores:
            data[field, pl.ds(line, 8), :] = value
        return carry

    lax.fori_loop(0, -(-count // unroll), body, 0)


def first_kernel(block_ref, even_ref, odd_ref, *state):
    data, words = state[:2]
    low_half = lane_ids() < LANES // 2
    is_even = lax.rem(lax.axis_index("gx"), 2) == 0
    even_line = jnp.where(is_even, row_line(8), row_line(-8))
    odd_line = jnp.where(is_even, row_line(-8), row_line(8))

    def get(field, lines):
        return data[field, lines, :] if field < 4 else words[lines, :]

    def put(field, lines, value):
        if field < 4:
            data[field, lines, :] = value
        else:
            words[lines, :] = value

    for field in range(FIELDS):
        for part in range(PITCH):
            source = pl.ds(field * BLOCK + 8 * part, 8)
            for ref, line in (
                (block_ref, row_line(0)), (even_ref, even_line), (odd_ref, odd_line)
            ):
                value = ref[source, :]
                if field == 4:
                    value = value.astype(jnp.int32)
                put(field, pl.ds(line + 8 * part, 8), value)
    for field in range(FIELDS):
        firsts = [row_line(row) for row in (-8, 0, 8)]
        heads = [get(field, pl.ds(line, 8, stride=PITCH)) for line in firsts]
        below = [get(field, pl.ds(line - PITCH, 8, stride=PITCH)) for line in firsts]
        final = get(field, pl.ds(row_line(15), 1))
        for line, head, last in zip(firsts, heads, below):
            put(field, pl.ds(line, 8, stride=PITCH), jnp.where(low_half, last, head))
        put(field, pl.ds(row_line(16), 1), final)
    first, last = row_line(-5), row_line(16)
    count = -(-(last - first) // 8)
    mask_lines(state, first, count, row_line(-8), 28)
    prepare_lines(state, row_line(-8), 5)
    force_lines(state, first, count)


def rest_kernel(below_ref, above_ref, *refs):
    count = len(refs) - 3
    state_count = count // 2
    disp_ref, vel_ref = refs[state_count : state_count + 2]
    state = refs[state_count + 2 : -1]
    over = refs[-1]
    data, words = state[:2]
    low = lax.broadcasted_iota(jnp.int32, (1, LANES), 1) < LANES // 2
    for field in range(FIELDS):
        below = below_ref[pl.ds(PITCH * field, PITCH), :]
        above = above_ref[pl.ds(PITCH * field, PITCH), :]
        if field == 4:
            below, above = below.astype(jnp.int32), above.astype(jnp.int32)
        target = data.at[field] if field < 4 else words
        target[pl.ds(row_line(-9), PITCH), :] = below
        head = pl.ds(row_line(-8), 1)
        target[head, :] = jnp.where(low, below[:1], target[head, :])
        head = pl.ds(row_line(16), 1)
        kept = target[head, :]
        target[pl.ds(row_line(16), PITCH), :] = above
        target[head, :] = jnp.where(low, kept, above[:1])
        target[pl.ds(row_line(17), 1), :] = above[:1]
    mask_lines(state, row_line(-6), 2, row_line(-9), 4)
    mask_lines(state, row_line(16), 2, row_line(15), 4)
    prepare_lines(state, row_line(-9), 5)
    force_lines(state, row_line(-6), 2)
    prepare_lines(state, row_line(15), 3)
    force_lines(state, row_line(16), 2)
    for which in range(3):
        reach = 3 * (2 - which)
        low_row, high_row = -reach, ROWS + reach
        first, last = row_line(low_row), row_line(high_row + 3) + 1
        if which:
            prepare_lines(state, row_line(low_row - 3), 5)
            force_lines(state, first, -(-(last - first) // 8))
        last = row_line(high_row) + 1
        update_lines(state, over, first, -(-(last - first) // 8), which, (4, 4, 3)[which])
    for tile in range(ROWS):
        lines = pl.ds(row_line(0) + 1 + tile, ROWS, stride=PITCH)
        cols = pl.ds(tile * LANES, LANES)
        for part in range(2):
            disp_ref[part, :, cols] = data[part, lines, :]
            vel_ref[part, :, cols] = data[2 + part, lines, :]


def shift(array, axis, by):
    count = lax.axis_size(axis)
    return lax.ppermute(array, axis, [(i, (i + by) % count) for i in range(count)])


def swap(array, axis, odd):
    count = lax.axis_size(axis)
    pairs = []
    for i in range(odd, count + odd, 2):
        pairs += [(i % count, (i + 1) % count), ((i + 1) % count, i % count)]
    return lax.ppermute(array, axis, pairs)


VMEM = pl.BlockSpec(memory_space=pltpu.VMEM)


def per_device(disp, vel, bonds):
    f32 = jnp.float32
    small = pltpu.CompilerParams(vmem_limit_bytes=4 * 2**20)
    paced = pltpu.CompilerParams(
        vmem_limit_bytes=4 * 2**20,
    )
    edge, disp, vel, bonds = pl.pallas_call(
        edge_kernel,
        out_shape=(
            jax.ShapeDtypeStruct((8 * FIELDS, LANES), f32),
            jax.ShapeDtypeStruct(disp.shape, disp.dtype),
            jax.ShapeDtypeStruct(vel.shape, vel.dtype),
            jax.ShapeDtypeStruct(bonds.shape, bonds.dtype),
        ),
        in_specs=[pl.BlockSpec(memory_space=pltpu.HBM)] * 3,
        out_specs=(VMEM,) * 4,
        scratch_shapes=[pltpu.SemaphoreType.DMA((3,))],
        compiler_params=small,
        name="edge",
    )(*(pltpu.with_memory_space_constraint(x, pltpu.HBM) for x in (disp, vel, bonds)))
    odd_edge = swap(edge, "gy", 1)
    even_edge = swap(edge, "gy", 0)
    ends = jax.ShapeDtypeStruct((FIELDS * PITCH, LANES), f32)
    block, first, last = pl.pallas_call(
        block_kernel,
        out_shape=(jax.ShapeDtypeStruct((FIELDS * BLOCK, LANES), f32), ends, ends),
        in_specs=[VMEM] * 5,
        out_specs=(VMEM,) * 3,
        compiler_params=small,
        name="block",
    )(disp, vel, bonds, even_edge, odd_edge)
    odd_block = swap(block, "gx", 1)
    even_block = swap(block, "gx", 0)
    below = shift(last, "gx", 2)
    above = shift(first, "gx", -2)
    work = (
        jax.ShapeDtypeStruct((4, LINES, LANES), f32),
        jax.ShapeDtypeStruct((LINES, LANES), jnp.int32),
        jax.ShapeDtypeStruct((12, LINES, LANES), f32),
        jax.ShapeDtypeStruct((3, LINES, LANES), jnp.int32),
        jax.ShapeDtypeStruct((24, LINES, LANES), f32),
        jax.ShapeDtypeStruct((8, LINES, LANES), f32),
        jax.ShapeDtypeStruct((26, LINES, LANES), f32),
    )
    state = pl.pallas_call(
        first_kernel,
        out_shape=work,
        in_specs=[VMEM] * 3,
        out_specs=(VMEM,) * len(work),
        compiler_params=paced,
        cost_estimate=pl.CostEstimate(
            flops=20_000_000, bytes_accessed=8_000_000, transcendentals=500_000
        ),
        name="first",
    )(block, even_block, odd_block)
    out = jax.ShapeDtypeStruct(disp.shape, f32)
    results = pl.pallas_call(
        rest_kernel,
        out_shape=(out, out) + work,
        in_specs=[VMEM] * (2 + len(work)),
        out_specs=(VMEM,) * (2 + len(work)),
        scratch_shapes=[pltpu.VMEM((2, LINES, LANES), f32)],
        input_output_aliases={2 + k: 2 + k for k in range(len(work))},
        compiler_params=paced,
        name="rest",
    )(below, above, *state)
    return results[0], results[1]


def solution(mesh):
    spec = P(None, "gx", "gy")
    return jax.shard_map(
        per_device,
        mesh=mesh,
        in_specs=(spec, spec, spec),
        out_specs=(spec, spec),
        check_vma=False,
    )
```

```python
import math

import jax
import jax.numpy as jnp
from jax import lax
from jax.experimental import pallas as pl
from jax.experimental.pallas import tpu as pltpu
from jax.sharding import PartitionSpec as P

STIFFNESS = 40.0
TIME_STEP = 0.05
SOFTENING = 0.0625
PACK_SHIFT = (0, 3, 10, 17)
LANES = 128

ROWS = 8
PITCH = 9
BLOCK = ROWS * PITCH
FIELDS = 5
HALO = 9
GUARD = 8
LINES = 272
LAG = 40


def row_line(row):
    return GUARD + PITCH * (row + HALO)


def lane_ids():
    return lax.broadcasted_iota(jnp.int32, (8, LANES), 1)


def edge_kernel(disp_hbm, vel_hbm, bonds_hbm, edge_ref, disp, vel, bonds, sems):
    copies = [
        pltpu.make_async_copy(source, target, sems.at[k])
        for k, (source, target) in enumerate(
            ((disp_hbm, disp), (vel_hbm, vel), (bonds_hbm, bonds))
        )
    ]
    for copy in copies:
        copy.start()
    for copy in copies:
        copy.wait()
    low_half = lane_ids() < LANES // 2
    left = pl.ds(0, LANES)
    right = pl.ds((ROWS - 1) * LANES, LANES)

    def ends(ref, part):
        return jnp.where(low_half, ref[part, :, left], ref[part, :, right])

    for part in range(2):
        edge_ref[pl.ds(8 * part, 8), :] = ends(disp, part)
        edge_ref[pl.ds(8 * part + 16, 8), :] = ends(vel, part)
    edge_ref[pl.ds(32, 8), :] = packed([ends(bonds, word) for word in range(4)])


def packed(words):
    total = words[0]
    for word in (1, 2, 3):
        total = total + words[word] * (1 << PACK_SHIFT[word])
    return total.astype(jnp.float32)


def block_kernel(disp_ref, vel_ref, bonds_ref, even_ref, odd_ref, block_ref, first_ref, last_ref):
    low_half = lane_ids() < LANES // 2
    is_even = lax.rem(lax.axis_index("gy"), 2) == 0
    for field in range(FIELDS):
        even = even_ref[pl.ds(8 * field, 8), :]
        odd = odd_ref[pl.ds(8 * field, 8), :]
        from_right = jnp.where(is_even, even, odd)
        from_left = jnp.where(is_even, odd, even)
        lines = [jnp.where(low_half, from_right, from_left)]
        for tile in range(ROWS):
            cols = pl.ds(tile * LANES, LANES)
            if field < 2:
                lines.append(disp_ref[field, :, cols])
            elif field < 4:
                lines.append(vel_ref[field - 2, :, cols])
            else:
                lines.append(packed([bonds_ref[word, :, cols] for word in range(4)]))
        for k, value in enumerate(lines):
            block_ref[pl.ds(field * BLOCK + k, ROWS, stride=PITCH), :] = value
            first_ref[pl.ds(PITCH * field + k, 1), :] = value[:1]
            last_ref[pl.ds(PITCH * field + k, 1), :] = value[7:]


def look_ahead(data, ahead, line, lanes):
    here = [data[f, pl.ds(line, 8), :] for f in range(4)]
    after = [data[f, pl.ds(line + 1, 8), :] for f in range(4)]
    for by in (1, 2, 3):
        for f in range(4):
            value = pltpu.roll(jnp.where(lanes < by, after[f], here[f]), LANES - by, 1)
            if f == 1:
                value = value + float(by)
            ahead[4 * (by - 1) + f, pl.ds(line, 8), :] = value


def prepare_lines(state, start, count):
    lanes = lane_ids()
    for step in range(count):
        look_ahead(state[0], state[2], start + 8 * step, lanes)


def mask_lines(state, start, count, ahead_start, ahead_count):
    _, words, _, ahead_words, masks = state[:5]
    lanes = lane_ids()
    for step in range(ahead_count):
        line = ahead_start + 8 * step
        here, after = words[pl.ds(line, 8), :], words[pl.ds(line + 1, 8), :]
        for by in (1, 2, 3):
            ahead_words[by - 1, pl.ds(line, 8), :] = pltpu.roll(
                jnp.where(lanes < by, after, here), LANES - by, 1
            )

    def body(step, carry):
        line = start + 8 * step

        def put(slot, row_off, col_off, word):
            weight = 1.0 / (row_off * row_off + col_off * col_off)
            masks[slot, pl.ds(line, 8), :] = jnp.where((word & (1 << slot)) != 0, weight, 0.0)

        for row_off in range(4):
            word = words[pl.ds(line - PITCH * row_off, 8), :]
            for col_off in range(4):
                if row_off == 0:
                    if col_off:
                        put(col_off - 1, row_off, col_off, word)
                    continue
                put(PACK_SHIFT[row_off] + col_off + 3, row_off, col_off, word)
                if col_off:
                    far_word = ahead_words[col_off - 1, pl.ds(line - PITCH * row_off, 8), :]
                    put(PACK_SHIFT[row_off] - col_off + 3, row_off, col_off, far_word)
        return carry

    lax.fori_loop(0, count, body, 0)


def bond_pull(far, near, row_off, col_off, mask):
    rest = math.sqrt(row_off * row_off + col_off * col_off + SOFTENING)
    along_x = far[0] - near[0]
    along_y = far[1] - near[1]
    rate_x = far[2] - near[2]
    rate_y = far[3] - near[3]
    inverse = lax.rsqrt(along_x * along_x + (along_y * along_y + SOFTENING))
    dot = along_x * rate_x + along_y * rate_y
    scale = mask * (STIFFNESS - (STIFFNESS * rest - dot * inverse) * inverse)
    return (scale * along_x, scale * along_y)


def added(total, value):
    if total is None:
        return list(value)
    return [total[part] + value[part] for part in range(2)]


def force_lines(state, start, count, carrying=True):
    data, _, ahead, _, masks, pull, push, over = state
    lanes = lane_ids()

    def body(step, carry):
        line = start + 8 * step
        here = [data[f, pl.ds(line, 8), :] for f in range(4)]
        found = [[ahead[4 * b + f, pl.ds(line, 8), :] for f in range(4)] for b in range(3)]
        look_ahead(data, ahead, line + 8, lanes)
        if carrying:
            carry_lines(push, over, line - LAG)

        def at(ref, k, offset):
            return ref[k, pl.ds(line - PITCH * offset, 8), :]

        def store(ref, k, value):
            for part in range(2):
                ref[2 * k + part, pl.ds(line, 8), :] = value[part]

        own = [None] * 4
        reach = [None] * 4
        for row_off in range(4):
            near = here if row_off == 0 else [at(data, f, row_off) for f in range(4)]
            if row_off:
                near[0] = near[0] - float(row_off)
            for col_off in range(4):
                if row_off == 0 and col_off == 0:
                    continue
                far = found[col_off - 1] if col_off else here
                slot = col_off - 1 if row_off == 0 else PACK_SHIFT[row_off] + col_off + 3
                mask = masks[slot, pl.ds(line, 8), :]
                value = bond_pull(far, near, row_off, col_off, mask)
                own[row_off] = added(own[row_off], value)
                reach[col_off] = added(reach[col_off], value)
        for col_off in range(4):
            store(push, col_off, reach[col_off])
        for row_off in (1, 2, 3):
            near = [here[0] + float(row_off)] + list(here[1:])
            for col_off in (1, 2, 3):
                far = [at(ahead, 4 * (col_off - 1) + f, row_off) for f in range(4)]
                slot = PACK_SHIFT[row_off] - col_off + 3
                mask = masks[slot, pl.ds(line, 8), :]
                value = bond_pull(far, near, row_off, col_off, mask)
                own[0] = added(own[0], value)
                store(push, 3 * row_off + col_off, value)
        for row_off in range(4):
            store(pull, row_off, own[row_off])
        return carry

    lax.fori_loop(0, count, body, 0)


def carry_lines(push, over, line):
    for part in range(2):
        for col_off in (1, 2, 3):
            total = push[2 * col_off + part, pl.ds(line, 8), :]
            for row_off in (1, 2, 3):
                slot = 2 * (3 * row_off + col_off) + part
                total = total + push[slot, pl.ds(line + PITCH * row_off, 8), :]
            over[2 * (col_off - 1) + part, pl.ds(line, 8), :] = pltpu.roll(total, col_off, 1)


def update_lines(state, start, count, which, unroll):
    data, _, _, _, _, pull, push, over = state
    lanes = lane_ids()

    def gain_at(line, part):
        def at(ref, k, offset):
            return ref[2 * k + part, pl.ds(line + offset, 8), :]

        force = at(pull, 0, 0) - at(push, 0, 0)
        for row_off in (1, 2, 3):
            force = force + at(pull, row_off, PITCH * row_off)
        for k in range(3):
            force = force - jnp.where(lanes > k, at(over, k, 0), at(over, k, -1))
        return (0.5 * TIME_STEP) * force

    def body(step, carry):
        stores = []
        for k in range(unroll):
            line = start + 8 * unroll * step + 8 * k
            for part in range(2):
                gain = gain_at(line, part)
                speed = data[2 + part, pl.ds(line, 8), :] + gain
                if which == 1:
                    speed = speed + gain
                stores.append((2 + part, line, speed))
                if which < 2:
                    moved = data[part, pl.ds(line, 8), :] + TIME_STEP * speed
                    stores.append((part, line, moved))
        for field, line, value in stores:
            data[field, pl.ds(line, 8), :] = value
        return carry

    lax.fori_loop(0, -(-count // unroll), body, 0)


def first_kernel(block_ref, even_ref, odd_ref, *state):
    data, words = state[:2]
    low_half = lane_ids() < LANES // 2
    is_even = lax.rem(lax.axis_index("gx"), 2) == 0
    even_line = jnp.where(is_even, row_line(8), row_line(-8))
    odd_line = jnp.where(is_even, row_line(-8), row_line(8))

    def get(field, lines):
        return data[field, lines, :] if field < 4 else words[lines, :]

    def put(field, lines, value):
        if field < 4:
            data[field, lines, :] = value
        else:
            words[lines, :] = value

    for field in range(FIELDS):
        for part in range(PITCH):
            source = pl.ds(field * BLOCK + 8 * part, 8)
            for ref, line in (
                (block_ref, row_line(0)), (even_ref, even_line), (odd_ref, odd_line)
            ):
                value = ref[source, :]
                if field == 4:
                    value = value.astype(jnp.int32)
                put(field, pl.ds(line + 8 * part, 8), value)
    for field in range(FIELDS):
        firsts = [row_line(row) for row in (-8, 0, 8)]
        heads = [get(field, pl.ds(line, 8, stride=PITCH)) for line in firsts]
        below = [get(field, pl.ds(line - PITCH, 8, stride=PITCH)) for line in firsts]
        final = get(field, pl.ds(row_line(15), 1))
        for line, head, last in zip(firsts, heads, below):
            put(field, pl.ds(line, 8, stride=PITCH), jnp.where(low_half, last, head))
        put(field, pl.ds(row_line(16), 1), final)
    first, last = row_line(-5), row_line(16)
    count = -(-(last - first) // 8)
    mask_lines(state, first, count, row_line(-8), 28)
    prepare_lines(state, row_line(-8), 5)
    force_lines(state, first, count)


def rest_kernel(below_ref, above_ref, *refs):
    state_count = (len(refs) - 2) // 2
    disp_ref, vel_ref = refs[state_count : state_count + 2]
    state = refs[state_count + 2 :]
    data, words = state[:2]
    push, over = state[6:]
    low = lax.broadcasted_iota(jnp.int32, (1, LANES), 1) < LANES // 2
    for field in range(FIELDS):
        below = below_ref[pl.ds(PITCH * field, PITCH), :]
        above = above_ref[pl.ds(PITCH * field, PITCH), :]
        if field == 4:
            below, above = below.astype(jnp.int32), above.astype(jnp.int32)
        target = data.at[field] if field < 4 else words
        target[pl.ds(row_line(-9), PITCH), :] = below
        head = pl.ds(row_line(-8), 1)
        target[head, :] = jnp.where(low, below[:1], target[head, :])
        head = pl.ds(row_line(16), 1)
        kept = target[head, :]
        target[pl.ds(row_line(16), PITCH), :] = above
        target[head, :] = jnp.where(low, kept, above[:1])
        target[pl.ds(row_line(17), 1), :] = above[:1]
    mask_lines(state, row_line(-6), 2, row_line(-9), 4)
    mask_lines(state, row_line(16), 2, row_line(15), 4)
    prepare_lines(state, row_line(-9), 5)
    force_lines(state, row_line(-6), 2, False)
    prepare_lines(state, row_line(15), 3)
    force_lines(state, row_line(16), 2, False)
    for line in (row_line(-6), row_line(-6) + 8):
        carry_lines(push, over, line)
    start, count = row_line(-5), -(-(row_line(16) - row_line(-5)) // 8)
    for which in range(3):
        reach = 3 * (2 - which)
        low_row, high_row = -reach, ROWS + reach
        first, last = row_line(low_row), row_line(high_row + 3) + 1
        if which:
            prepare_lines(state, row_line(low_row - 3), 5)
            start, count = first, -(-(last - first) // 8)
            force_lines(state, start, count)
        last = row_line(high_row) + 1
        for line in range(start + 8 * count - LAG, last, 8):
            carry_lines(push, over, line)
        update_lines(state, first, -(-(last - first) // 8), which, (4, 4, 3)[which])
    for tile in range(ROWS):
        lines = pl.ds(row_line(0) + 1 + tile, ROWS, stride=PITCH)
        cols = pl.ds(tile * LANES, LANES)
        for part in range(2):
            disp_ref[part, :, cols] = data[part, lines, :]
            vel_ref[part, :, cols] = data[2 + part, lines, :]


def shift(array, axis, by):
    count = lax.axis_size(axis)
    return lax.ppermute(array, axis, [(i, (i + by) % count) for i in range(count)])


def swap(array, axis, odd):
    count = lax.axis_size(axis)
    pairs = []
    for i in range(odd, count + odd, 2):
        pairs += [(i % count, (i + 1) % count), ((i + 1) % count, i % count)]
    return lax.ppermute(array, axis, pairs)


VMEM = pl.BlockSpec(memory_space=pltpu.VMEM)


def per_device(disp, vel, bonds):
    f32 = jnp.float32
    small = pltpu.CompilerParams(vmem_limit_bytes=4 * 2**20)
    paced = pltpu.CompilerParams(
        vmem_limit_bytes=4 * 2**20,
    )
    edge, disp, vel, bonds = pl.pallas_call(
        edge_kernel,
        out_shape=(
            jax.ShapeDtypeStruct((8 * FIELDS, LANES), f32),
            jax.ShapeDtypeStruct(disp.shape, disp.dtype),
            jax.ShapeDtypeStruct(vel.shape, vel.dtype),
            jax.ShapeDtypeStruct(bonds.shape, bonds.dtype),
        ),
        in_specs=[pl.BlockSpec(memory_space=pltpu.HBM)] * 3,
        out_specs=(VMEM,) * 4,
        scratch_shapes=[pltpu.SemaphoreType.DMA((3,))],
        compiler_params=small,
        name="edge",
    )(*(pltpu.with_memory_space_constraint(x, pltpu.HBM) for x in (disp, vel, bonds)))
    odd_edge = swap(edge, "gy", 1)
    even_edge = swap(edge, "gy", 0)
    ends = jax.ShapeDtypeStruct((FIELDS * PITCH, LANES), f32)
    block, first, last = pl.pallas_call(
        block_kernel,
        out_shape=(jax.ShapeDtypeStruct((FIELDS * BLOCK, LANES), f32), ends, ends),
        in_specs=[VMEM] * 5,
        out_specs=(VMEM,) * 3,
        compiler_params=small,
        name="block",
    )(disp, vel, bonds, even_edge, odd_edge)
    odd_block = swap(block, "gx", 1)
    even_block = swap(block, "gx", 0)
    below = shift(last, "gx", 2)
    above = shift(first, "gx", -2)
    work = (
        jax.ShapeDtypeStruct((4, LINES, LANES), f32),
        jax.ShapeDtypeStruct((LINES, LANES), jnp.int32),
        jax.ShapeDtypeStruct((12, LINES, LANES), f32),
        jax.ShapeDtypeStruct((3, LINES, LANES), jnp.int32),
        jax.ShapeDtypeStruct((24, LINES, LANES), f32),
        jax.ShapeDtypeStruct((8, LINES, LANES), f32),
        jax.ShapeDtypeStruct((26, LINES, LANES), f32),
        jax.ShapeDtypeStruct((6, LINES, LANES), f32),
    )
    state = pl.pallas_call(
        first_kernel,
        out_shape=work,
        in_specs=[VMEM] * 3,
        out_specs=(VMEM,) * len(work),
        compiler_params=paced,
        cost_estimate=pl.CostEstimate(
            flops=20_000_000, bytes_accessed=8_000_000, transcendentals=500_000
        ),
        name="first",
    )(block, even_block, odd_block)
    out = jax.ShapeDtypeStruct(disp.shape, f32)
    results = pl.pallas_call(
        rest_kernel,
        out_shape=(out, out) + work,
        in_specs=[VMEM] * (2 + len(work)),
        out_specs=(VMEM,) * (2 + len(work)),
        input_output_aliases={2 + k: 2 + k for k in range(len(work))},
        compiler_params=paced,
        name="rest",
    )(below, above, *state)
    return results[0], results[1]


def solution(mesh):
    spec = P(None, "gx", "gy")
    return jax.shard_map(
        per_device,
        mesh=mesh,
        in_specs=(spec, spec, spec),
        out_specs=(spec, spec),
        check_vma=False,
    )
```

```python
import math

import jax
import jax.numpy as jnp
from jax import lax
from jax.experimental import pallas as pl
from jax.experimental.pallas import tpu as pltpu
from jax.sharding import PartitionSpec as P

STIFFNESS = 40.0
TIME_STEP = 0.05
SOFTENING = 0.0625
PACK_SHIFT = (0, 3, 10, 17)
LANES = 128

ROWS = 8
PITCH = 9
BLOCK = ROWS * PITCH
FIELDS = 5
HALO = 9
GUARD = 16
LINES = 280
LAG = 40


def row_line(row):
    return GUARD + PITCH * (row + HALO)


def lane_ids():
    return lax.broadcasted_iota(jnp.int32, (8, LANES), 1)


def edge_kernel(disp_hbm, vel_hbm, bonds_hbm, edge_ref, disp, vel, bonds, sems):
    copies = [
        pltpu.make_async_copy(source, target, sems.at[k])
        for k, (source, target) in enumerate(
            ((disp_hbm, disp), (vel_hbm, vel), (bonds_hbm, bonds))
        )
    ]
    for copy in copies:
        copy.start()
    for copy in copies:
        copy.wait()
    low_half = lane_ids() < LANES // 2
    left = pl.ds(0, LANES)
    right = pl.ds((ROWS - 1) * LANES, LANES)

    def ends(ref, part):
        return jnp.where(low_half, ref[part, :, left], ref[part, :, right])

    for part in range(2):
        edge_ref[pl.ds(8 * part, 8), :] = ends(disp, part)
        edge_ref[pl.ds(8 * part + 16, 8), :] = ends(vel, part)
    edge_ref[pl.ds(32, 8), :] = packed([ends(bonds, word) for word in range(4)])


def packed(words):
    total = words[0]
    for word in (1, 2, 3):
        total = total + words[word] * (1 << PACK_SHIFT[word])
    return total.astype(jnp.float32)


def block_kernel(disp_ref, vel_ref, bonds_ref, even_ref, odd_ref, block_ref, first_ref, last_ref):
    low_half = lane_ids() < LANES // 2
    is_even = lax.rem(lax.axis_index("gy"), 2) == 0
    for field in range(FIELDS):
        even = even_ref[pl.ds(8 * field, 8), :]
        odd = odd_ref[pl.ds(8 * field, 8), :]
        from_right = jnp.where(is_even, even, odd)
        from_left = jnp.where(is_even, odd, even)
        lines = [jnp.where(low_half, from_right, from_left)]
        for tile in range(ROWS):
            cols = pl.ds(tile * LANES, LANES)
            if field < 2:
                lines.append(disp_ref[field, :, cols])
            elif field < 4:
                lines.append(vel_ref[field - 2, :, cols])
            else:
                lines.append(packed([bonds_ref[word, :, cols] for word in range(4)]))
        for k, value in enumerate(lines):
            block_ref[pl.ds(field * BLOCK + k, ROWS, stride=PITCH), :] = value
            first_ref[pl.ds(PITCH * field + k, 1), :] = value[:1]
            last_ref[pl.ds(PITCH * field + k, 1), :] = value[7:]


def look_ahead(data, ahead, line, lanes):
    here = [data[f, pl.ds(line, 8), :] for f in range(4)]
    after = [data[f, pl.ds(line + 1, 8), :] for f in range(4)]
    for by in (1, 2, 3):
        for f in range(4):
            value = pltpu.roll(jnp.where(lanes < by, after[f], here[f]), LANES - by, 1)
            if f == 1:
                value = value + float(by)
            ahead[4 * (by - 1) + f, pl.ds(line, 8), :] = value


def prepare_lines(state, start, count):
    lanes = lane_ids()
    for step in range(count):
        look_ahead(state[0], state[2], start + 8 * step, lanes)


def mask_lines(state, start, count, ahead_start, ahead_count):
    _, words, _, ahead_words, masks = state[:5]
    lanes = lane_ids()
    for step in range(ahead_count):
        line = ahead_start + 8 * step
        here, after = words[pl.ds(line, 8), :], words[pl.ds(line + 1, 8), :]
        for by in (1, 2, 3):
            ahead_words[by - 1, pl.ds(line, 8), :] = pltpu.roll(
                jnp.where(lanes < by, after, here), LANES - by, 1
            )

    def body(step, carry):
        line = start + 8 * step

        def put(slot, row_off, col_off, word):
            weight = 1.0 / (row_off * row_off + col_off * col_off)
            masks[slot, pl.ds(line, 8), :] = jnp.where((word & (1 << slot)) != 0, weight, 0.0)

        for row_off in range(4):
            word = words[pl.ds(line - PITCH * row_off, 8), :]
            for col_off in range(4):
                if row_off == 0:
                    if col_off:
                        put(col_off - 1, row_off, col_off, word)
                    continue
                put(PACK_SHIFT[row_off] + col_off + 3, row_off, col_off, word)
                if col_off:
                    far_word = ahead_words[col_off - 1, pl.ds(line - PITCH * row_off, 8), :]
                    put(PACK_SHIFT[row_off] - col_off + 3, row_off, col_off, far_word)
        return carry

    lax.fori_loop(0, count, body, 0)


def bond_pull(far, near, row_off, col_off, mask):
    rest = math.sqrt(row_off * row_off + col_off * col_off + SOFTENING)
    along_x = far[0] - near[0]
    along_y = far[1] - near[1]
    rate_x = far[2] - near[2]
    rate_y = far[3] - near[3]
    inverse = lax.rsqrt(along_x * along_x + (along_y * along_y + SOFTENING))
    dot = along_x * rate_x + along_y * rate_y
    scale = mask * (STIFFNESS - (STIFFNESS * rest - dot * inverse) * inverse)
    return (scale * along_x, scale * along_y)


def added(total, value):
    if total is None:
        return list(value)
    return [total[part] + value[part] for part in range(2)]


def force_lines(state, start, count, carrying=True):
    data, _, ahead, _, masks, pull, push, over = state
    lanes = lane_ids()

    def body(step, carry):
        line = start + 8 * step
        here = [data[f, pl.ds(line, 8), :] for f in range(4)]
        found = [[ahead[4 * b + f, pl.ds(line, 8), :] for f in range(4)] for b in range(3)]
        look_ahead(data, ahead, line + 8, lanes)
        if carrying:
            carry_lines(push, over, line - LAG)

        def at(ref, k, offset):
            return ref[k, pl.ds(line - PITCH * offset, 8), :]

        def store(ref, k, value):
            for part in range(2):
                ref[2 * k + part, pl.ds(line, 8), :] = value[part]

        own = [None] * 4
        reach = [None] * 4
        for row_off in range(4):
            near = here if row_off == 0 else [at(data, f, row_off) for f in range(4)]
            if row_off:
                near[0] = near[0] - float(row_off)
            for col_off in range(4):
                if row_off == 0 and col_off == 0:
                    continue
                far = found[col_off - 1] if col_off else here
                slot = col_off - 1 if row_off == 0 else PACK_SHIFT[row_off] + col_off + 3
                mask = masks[slot, pl.ds(line, 8), :]
                value = bond_pull(far, near, row_off, col_off, mask)
                own[row_off] = added(own[row_off], value)
                reach[col_off] = added(reach[col_off], value)
        for col_off in range(4):
            store(push, col_off, reach[col_off])
        for row_off in (1, 2, 3):
            near = [here[0] + float(row_off)] + list(here[1:])
            for col_off in (1, 2, 3):
                far = [at(ahead, 4 * (col_off - 1) + f, row_off) for f in range(4)]
                slot = PACK_SHIFT[row_off] - col_off + 3
                mask = masks[slot, pl.ds(line, 8), :]
                value = bond_pull(far, near, row_off, col_off, mask)
                own[0] = added(own[0], value)
                store(push, 3 * row_off + col_off, value)
        for row_off in range(4):
            store(pull, row_off, own[row_off])
        return carry

    lax.fori_loop(0, count, body, 0)


def carry_lines(push, over, line):
    for part in range(2):
        for col_off in (1, 2, 3):
            total = push[2 * col_off + part, pl.ds(line, 8), :]
            for row_off in (1, 2, 3):
                slot = 2 * (3 * row_off + col_off) + part
                total = total + push[slot, pl.ds(line + PITCH * row_off, 8), :]
            over[2 * (col_off - 1) + part, pl.ds(line, 8), :] = pltpu.roll(total, col_off, 1)


def update_lines(state, start, count, which, unroll):
    data, _, _, _, _, pull, push, over = state
    lanes = lane_ids()

    def gain_at(line, part):
        def at(ref, k, offset):
            return ref[2 * k + part, pl.ds(line + offset, 8), :]

        force = at(pull, 0, 0) - at(push, 0, 0)
        for row_off in (1, 2, 3):
            force = force + at(pull, row_off, PITCH * row_off)
        for k in range(3):
            force = force - jnp.where(lanes > k, at(over, k, 0), at(over, k, -1))
        return (0.5 * TIME_STEP) * force

    def body(step, carry):
        stores = []
        for k in range(unroll):
            line = start + 8 * unroll * step + 8 * k
            for part in range(2):
                gain = gain_at(line, part)
                speed = data[2 + part, pl.ds(line, 8), :] + gain
                if which == 1:
                    speed = speed + gain
                stores.append((2 + part, line, speed))
                if which < 2:
                    moved = data[part, pl.ds(line, 8), :] + TIME_STEP * speed
                    stores.append((part, line, moved))
        for field, line, value in stores:
            data[field, pl.ds(line, 8), :] = value
        return carry

    lax.fori_loop(0, -(-count // unroll), body, 0)


def first_kernel(block_ref, even_ref, odd_ref, below_ref, *state):
    data, words = state[:2]
    low_half = lane_ids() < LANES // 2
    is_even = lax.rem(lax.axis_index("gx"), 2) == 0
    even_line = jnp.where(is_even, row_line(8), row_line(-8))
    odd_line = jnp.where(is_even, row_line(-8), row_line(8))

    def get(field, lines):
        return data[field, lines, :] if field < 4 else words[lines, :]

    def put(field, lines, value):
        if field < 4:
            data[field, lines, :] = value
        else:
            words[lines, :] = value

    for field in range(FIELDS):
        for part in range(PITCH):
            source = pl.ds(field * BLOCK + 8 * part, 8)
            for ref, line in (
                (block_ref, row_line(0)), (even_ref, even_line), (odd_ref, odd_line)
            ):
                value = ref[source, :]
                if field == 4:
                    value = value.astype(jnp.int32)
                put(field, pl.ds(line + 8 * part, 8), value)
        value = below_ref[pl.ds(PITCH * field, PITCH), :]
        if field == 4:
            value = value.astype(jnp.int32)
        put(field, pl.ds(row_line(-9), PITCH), value)
    for field in range(FIELDS):
        firsts = [row_line(row) for row in (-8, 0, 8)]
        heads = [get(field, pl.ds(line, 8, stride=PITCH)) for line in firsts]
        below = [get(field, pl.ds(line - PITCH, 8, stride=PITCH)) for line in firsts]
        final = get(field, pl.ds(row_line(15), 1))
        for line, head, last in zip(firsts, heads, below):
            put(field, pl.ds(line, 8, stride=PITCH), jnp.where(low_half, last, head))
        put(field, pl.ds(row_line(16), 1), final)
    first, last = row_line(-6), row_line(16)
    count = -(-(last - first) // 8)
    mask_lines(state, first, count, row_line(-9), 28)
    prepare_lines(state, row_line(-9), 5)
    force_lines(state, first, count)


def rest_kernel(above_ref, *refs):
    state_count = (len(refs) - 2) // 2
    disp_ref, vel_ref = refs[state_count : state_count + 2]
    state = refs[state_count + 2 :]
    data, words = state[:2]
    push, over = state[6:]
    low = lax.broadcasted_iota(jnp.int32, (1, LANES), 1) < LANES // 2
    for field in range(FIELDS):
        above = above_ref[pl.ds(PITCH * field, PITCH), :]
        if field == 4:
            above = above.astype(jnp.int32)
        target = data.at[field] if field < 4 else words
        head = pl.ds(row_line(16), 1)
        kept = target[head, :]
        target[pl.ds(row_line(16), PITCH), :] = above
        target[head, :] = jnp.where(low, kept, above[:1])
        target[pl.ds(row_line(17), 1), :] = above[:1]
    mask_lines(state, row_line(16), 2, row_line(16) - 1, 1)
    prepare_lines(state, row_line(16), 1)
    force_lines(state, row_line(16), 2, False)
    start, count = row_line(-6), -(-(row_line(16) - row_line(-6)) // 8)
    for which in range(3):
        reach = 3 * (2 - which)
        low_row, high_row = -reach, ROWS + reach
        first, last = row_line(low_row), row_line(high_row + 3) + 1
        if which:
            prepare_lines(state, row_line(low_row - 3), 5)
            start, count = first, -(-(last - first) // 8)
            force_lines(state, start, count)
        last = row_line(high_row) + 1
        for line in range(start + 8 * count - LAG, last, 8):
            carry_lines(push, over, line)
        update_lines(state, first, -(-(last - first) // 8), which, (4, 4, 3)[which])
    for tile in range(ROWS):
        lines = pl.ds(row_line(0) + 1 + tile, ROWS, stride=PITCH)
        cols = pl.ds(tile * LANES, LANES)
        for part in range(2):
            disp_ref[part, :, cols] = data[part, lines, :]
            vel_ref[part, :, cols] = data[2 + part, lines, :]


def shift(array, axis, by):
    count = lax.axis_size(axis)
    return lax.ppermute(array, axis, [(i, (i + by) % count) for i in range(count)])


def swap(array, axis, odd):
    count = lax.axis_size(axis)
    pairs = []
    for i in range(odd, count + odd, 2):
        pairs += [(i % count, (i + 1) % count), ((i + 1) % count, i % count)]
    return lax.ppermute(array, axis, pairs)


VMEM = pl.BlockSpec(memory_space=pltpu.VMEM)


def per_device(disp, vel, bonds):
    f32 = jnp.float32
    small = pltpu.CompilerParams(vmem_limit_bytes=4 * 2**20)
    paced = pltpu.CompilerParams(
        vmem_limit_bytes=4 * 2**20,
    )
    edge, disp, vel, bonds = pl.pallas_call(
        edge_kernel,
        out_shape=(
            jax.ShapeDtypeStruct((8 * FIELDS, LANES), f32),
            jax.ShapeDtypeStruct(disp.shape, disp.dtype),
            jax.ShapeDtypeStruct(vel.shape, vel.dtype),
            jax.ShapeDtypeStruct(bonds.shape, bonds.dtype),
        ),
        in_specs=[pl.BlockSpec(memory_space=pltpu.HBM)] * 3,
        out_specs=(VMEM,) * 4,
        scratch_shapes=[pltpu.SemaphoreType.DMA((3,))],
        compiler_params=small,
        name="edge",
    )(*(pltpu.with_memory_space_constraint(x, pltpu.HBM) for x in (disp, vel, bonds)))
    odd_edge = swap(edge, "gy", 1)
    even_edge = swap(edge, "gy", 0)
    ends = jax.ShapeDtypeStruct((FIELDS * PITCH, LANES), f32)
    block, first, last = pl.pallas_call(
        block_kernel,
        out_shape=(jax.ShapeDtypeStruct((FIELDS * BLOCK, LANES), f32), ends, ends),
        in_specs=[VMEM] * 5,
        out_specs=(VMEM,) * 3,
        compiler_params=small,
        name="block",
    )(disp, vel, bonds, even_edge, odd_edge)
    odd_block = swap(block, "gx", 1)
    even_block = swap(block, "gx", 0)
    below = shift(last, "gx", 2)
    above = shift(first, "gx", -2)
    work = (
        jax.ShapeDtypeStruct((4, LINES, LANES), f32),
        jax.ShapeDtypeStruct((LINES, LANES), jnp.int32),
        jax.ShapeDtypeStruct((12, LINES, LANES), f32),
        jax.ShapeDtypeStruct((3, LINES, LANES), jnp.int32),
        jax.ShapeDtypeStruct((24, LINES, LANES), f32),
        jax.ShapeDtypeStruct((8, LINES, LANES), f32),
        jax.ShapeDtypeStruct((26, LINES, LANES), f32),
        jax.ShapeDtypeStruct((6, LINES, LANES), f32),
    )
    state = pl.pallas_call(
        first_kernel,
        out_shape=work,
        in_specs=[VMEM] * 4,
        out_specs=(VMEM,) * len(work),
        compiler_params=paced,
        cost_estimate=pl.CostEstimate(
            flops=20_000_000, bytes_accessed=8_000_000, transcendentals=500_000
        ),
        name="first",
    )(block, even_block, odd_block, below)
    out = jax.ShapeDtypeStruct(disp.shape, f32)
    results = pl.pallas_call(
        rest_kernel,
        out_shape=(out, out) + work,
        in_specs=[VMEM] * (1 + len(work)),
        out_specs=(VMEM,) * (2 + len(work)),
        input_output_aliases={1 + k: 2 + k for k in range(len(work))},
        compiler_params=paced,
        name="rest",
    )(above, *state)
    return results[0], results[1]


def solution(mesh):
    spec = P(None, "gx", "gy")
    return jax.shard_map(
        per_device,
        mesh=mesh,
        in_specs=(spec, spec, spec),
        out_specs=(spec, spec),
        check_vma=False,
    )
```

```python
import math

import jax
import jax.numpy as jnp
from jax import lax
from jax.experimental import pallas as pl
from jax.experimental.pallas import tpu as pltpu
from jax.sharding import PartitionSpec as P

STIFFNESS = 40.0
TIME_STEP = 0.05
SOFTENING = 0.0625
PACK_SHIFT = (0, 3, 10, 17)
LANES = 128

ROWS = 8
PITCH = 9
BLOCK = ROWS * PITCH
FIELDS = 5
HALO = 9
GUARD = 16
LINES = 280
LAG = 40


def row_line(row):
    return GUARD + PITCH * (row + HALO)


def lane_ids():
    return lax.broadcasted_iota(jnp.int32, (8, LANES), 1)


def edge_kernel(disp_hbm, vel_hbm, bonds_hbm, edge_ref, disp, vel, bonds, sems):
    copies = [
        pltpu.make_async_copy(source, target, sems.at[k])
        for k, (source, target) in enumerate(
            ((disp_hbm, disp), (vel_hbm, vel), (bonds_hbm, bonds))
        )
    ]
    for copy in copies:
        copy.start()
    for copy in copies:
        copy.wait()
    low_half = lane_ids() < LANES // 2
    left = pl.ds(0, LANES)
    right = pl.ds((ROWS - 1) * LANES, LANES)

    def ends(ref, part):
        return jnp.where(low_half, ref[part, :, left], ref[part, :, right])

    for part in range(2):
        edge_ref[pl.ds(8 * part, 8), :] = ends(disp, part)
        edge_ref[pl.ds(8 * part + 16, 8), :] = ends(vel, part)
    edge_ref[pl.ds(32, 8), :] = packed([ends(bonds, word) for word in range(4)])


def packed(words):
    total = words[0]
    for word in (1, 2, 3):
        total = total + words[word] * (1 << PACK_SHIFT[word])
    return total.astype(jnp.float32)


def block_kernel(disp_ref, vel_ref, bonds_ref, even_ref, odd_ref, block_ref, first_ref, last_ref):
    low_half = lane_ids() < LANES // 2
    is_even = lax.rem(lax.axis_index("gy"), 2) == 0
    for field in range(FIELDS):
        even = even_ref[pl.ds(8 * field, 8), :]
        odd = odd_ref[pl.ds(8 * field, 8), :]
        from_right = jnp.where(is_even, even, odd)
        from_left = jnp.where(is_even, odd, even)
        lines = [jnp.where(low_half, from_right, from_left)]
        for tile in range(ROWS):
            cols = pl.ds(tile * LANES, LANES)
            if field < 2:
                lines.append(disp_ref[field, :, cols])
            elif field < 4:
                lines.append(vel_ref[field - 2, :, cols])
            else:
                lines.append(packed([bonds_ref[word, :, cols] for word in range(4)]))
        for k, value in enumerate(lines):
            block_ref[pl.ds(field * BLOCK + k, ROWS, stride=PITCH), :] = value
            first_ref[pl.ds(PITCH * field + k, 1), :] = value[:1]
            last_ref[pl.ds(PITCH * field + k, 1), :] = value[7:]


def look_ahead(data, ahead, line, lanes):
    here = [data[f, pl.ds(line, 8), :] for f in range(4)]
    after = [data[f, pl.ds(line + 1, 8), :] for f in range(4)]
    for by in (1, 2, 3):
        for f in range(4):
            value = pltpu.roll(jnp.where(lanes < by, after[f], here[f]), LANES - by, 1)
            if f == 1:
                value = value + float(by)
            ahead[4 * (by - 1) + f, pl.ds(line, 8), :] = value


def prepare_lines(state, start, count):
    lanes = lane_ids()
    for step in range(count):
        look_ahead(state[0], state[2], start + 8 * step, lanes)


def mask_lines(state, start, count, ahead_start, ahead_count):
    _, words, _, ahead_words, masks = state[:5]
    lanes = lane_ids()
    for step in range(ahead_count):
        line = ahead_start + 8 * step
        here, after = words[pl.ds(line, 8), :], words[pl.ds(line + 1, 8), :]
        for by in (1, 2, 3):
            ahead_words[by - 1, pl.ds(line, 8), :] = pltpu.roll(
                jnp.where(lanes < by, after, here), LANES - by, 1
            )

    def fill(line):
        def mask(slot, row_off, col_off, word):
            weight = 1.0 / (row_off * row_off + col_off * col_off)
            return slot, jnp.where((word & (1 << slot)) != 0, weight, 0.0)

        made = []
        for row_off in range(4):
            word = words[pl.ds(line - PITCH * row_off, 8), :]
            for col_off in range(4):
                if row_off == 0:
                    if col_off:
                        made.append(mask(col_off - 1, row_off, col_off, word))
                    continue
                made.append(mask(PACK_SHIFT[row_off] + col_off + 3, row_off, col_off, word))
                if col_off:
                    far_word = ahead_words[col_off - 1, pl.ds(line - PITCH * row_off, 8), :]
                    slot = PACK_SHIFT[row_off] - col_off + 3
                    made.append(mask(slot, row_off, col_off, far_word))
        for slot, value in made:
            masks[slot, pl.ds(line, 8), :] = value

    def body(step, carry):
        for k in range(2):
            fill(start + 16 * step + 8 * k)
        return carry

    lax.fori_loop(0, -(-count // 2), body, 0)


def bond_pull(far, near, row_off, col_off, mask):
    rest = math.sqrt(row_off * row_off + col_off * col_off + SOFTENING)
    along_x = far[0] - near[0]
    along_y = far[1] - near[1]
    rate_x = far[2] - near[2]
    rate_y = far[3] - near[3]
    inverse = lax.rsqrt(along_x * along_x + (along_y * along_y + SOFTENING))
    dot = along_x * rate_x + along_y * rate_y
    scale = mask * (STIFFNESS - (STIFFNESS * rest - dot * inverse) * inverse)
    return (scale * along_x, scale * along_y)


def added(total, value):
    if total is None:
        return list(value)
    return [total[part] + value[part] for part in range(2)]


def force_lines(state, start, count, carrying=True):
    data, _, ahead, _, masks, pull, push, over = state
    lanes = lane_ids()

    def body(step, carry):
        line = start + 8 * step
        here = [data[f, pl.ds(line, 8), :] for f in range(4)]
        found = [[ahead[4 * b + f, pl.ds(line, 8), :] for f in range(4)] for b in range(3)]
        look_ahead(data, ahead, line + 8, lanes)
        if carrying:
            carry_lines(push, over, line - LAG)

        def at(ref, k, offset):
            return ref[k, pl.ds(line - PITCH * offset, 8), :]

        def store(ref, k, value):
            for part in range(2):
                ref[2 * k + part, pl.ds(line, 8), :] = value[part]

        own = [None] * 4
        reach = [None] * 4
        for row_off in range(4):
            near = here if row_off == 0 else [at(data, f, row_off) for f in range(4)]
            if row_off:
                near[0] = near[0] - float(row_off)
            for col_off in range(4):
                if row_off == 0 and col_off == 0:
                    continue
                far = found[col_off - 1] if col_off else here
                slot = col_off - 1 if row_off == 0 else PACK_SHIFT[row_off] + col_off + 3
                mask = masks[slot, pl.ds(line, 8), :]
                value = bond_pull(far, near, row_off, col_off, mask)
                own[row_off] = added(own[row_off], value)
                reach[col_off] = added(reach[col_off], value)
        for col_off in range(4):
            store(push, col_off, reach[col_off])
        for row_off in (1, 2, 3):
            near = [here[0] + float(row_off)] + list(here[1:])
            for col_off in (1, 2, 3):
                far = [at(ahead, 4 * (col_off - 1) + f, row_off) for f in range(4)]
                slot = PACK_SHIFT[row_off] - col_off + 3
                mask = masks[slot, pl.ds(line, 8), :]
                value = bond_pull(far, near, row_off, col_off, mask)
                own[0] = added(own[0], value)
                store(push, 3 * row_off + col_off, value)
        for row_off in range(4):
            store(pull, row_off, own[row_off])
        return carry

    lax.fori_loop(0, count, body, 0)


def carry_lines(push, over, line):
    for part in range(2):
        for col_off in (1, 2, 3):
            total = push[2 * col_off + part, pl.ds(line, 8), :]
            for row_off in (1, 2, 3):
                slot = 2 * (3 * row_off + col_off) + part
                total = total + push[slot, pl.ds(line + PITCH * row_off, 8), :]
            over[2 * (col_off - 1) + part, pl.ds(line, 8), :] = pltpu.roll(total, col_off, 1)


def update_lines(state, start, count, which, unroll):
    data, _, _, _, _, pull, push, over = state
    lanes = lane_ids()

    def gain_at(line, part):
        def at(ref, k, offset):
            return ref[2 * k + part, pl.ds(line + offset, 8), :]

        force = at(pull, 0, 0) - at(push, 0, 0)
        for row_off in (1, 2, 3):
            force = force + at(pull, row_off, PITCH * row_off)
        for k in range(3):
            force = force - jnp.where(lanes > k, at(over, k, 0), at(over, k, -1))
        return (0.5 * TIME_STEP) * force

    def body(step, carry):
        stores = []
        for k in range(unroll):
            line = start + 8 * unroll * step + 8 * k
            for part in range(2):
                gain = gain_at(line, part)
                speed = data[2 + part, pl.ds(line, 8), :] + gain
                if which == 1:
                    speed = speed + gain
                stores.append((2 + part, line, speed))
                if which < 2:
                    moved = data[part, pl.ds(line, 8), :] + TIME_STEP * speed
                    stores.append((part, line, moved))
        for field, line, value in stores:
            data[field, pl.ds(line, 8), :] = value
        return carry

    lax.fori_loop(0, -(-count // unroll), body, 0)


def first_kernel(block_ref, even_ref, odd_ref, below_ref, *state):
    data, words = state[:2]
    low_half = lane_ids() < LANES // 2
    is_even = lax.rem(lax.axis_index("gx"), 2) == 0
    even_line = jnp.where(is_even, row_line(8), row_line(-8))
    odd_line = jnp.where(is_even, row_line(-8), row_line(8))

    def get(field, lines):
        return data[field, lines, :] if field < 4 else words[lines, :]

    def put(field, lines, value):
        if field < 4:
            data[field, lines, :] = value
        else:
            words[lines, :] = value

    for field in range(FIELDS):
        for part in range(PITCH):
            source = pl.ds(field * BLOCK + 8 * part, 8)
            for ref, line in (
                (block_ref, row_line(0)), (even_ref, even_line), (odd_ref, odd_line)
            ):
                value = ref[source, :]
                if field == 4:
                    value = value.astype(jnp.int32)
                put(field, pl.ds(line + 8 * part, 8), value)
        value = below_ref[pl.ds(PITCH * field, PITCH), :]
        if field == 4:
            value = value.astype(jnp.int32)
        put(field, pl.ds(row_line(-9), PITCH), value)
    for field in range(FIELDS):
        firsts = [row_line(row) for row in (-8, 0, 8)]
        heads = [get(field, pl.ds(line, 8, stride=PITCH)) for line in firsts]
        below = [get(field, pl.ds(line - PITCH, 8, stride=PITCH)) for line in firsts]
        final = get(field, pl.ds(row_line(15), 1))
        for line, head, last in zip(firsts, heads, below):
            put(field, pl.ds(line, 8, stride=PITCH), jnp.where(low_half, last, head))
        put(field, pl.ds(row_line(16), 1), final)
    first, last = row_line(-6), row_line(16)
    count = -(-(last - first) // 8)
    mask_lines(state, first, count, row_line(-9), 28)
    prepare_lines(state, row_line(-9), 5)
    force_lines(state, first, count)


def rest_kernel(above_ref, *refs):
    *refs, moved, sem = refs
    state_count = (len(refs) - 2) // 2
    disp_ref, vel_ref = refs[state_count : state_count + 2]
    state = refs[state_count + 2 :]
    data, words = state[:2]
    push, over = state[6:]
    low = lax.broadcasted_iota(jnp.int32, (1, LANES), 1) < LANES // 2
    for field in range(FIELDS):
        above = above_ref[pl.ds(PITCH * field, PITCH), :]
        if field == 4:
            above = above.astype(jnp.int32)
        target = data.at[field] if field < 4 else words
        head = pl.ds(row_line(16), 1)
        kept = target[head, :]
        target[pl.ds(row_line(16), PITCH), :] = above
        target[head, :] = jnp.where(low, kept, above[:1])
        target[pl.ds(row_line(17), 1), :] = above[:1]
    mask_lines(state, row_line(16), 2, row_line(16) - 1, 1)
    prepare_lines(state, row_line(16), 1)
    force_lines(state, row_line(16), 2, False)
    copy = pltpu.make_async_copy(moved, disp_ref, sem)
    start, count = row_line(-6), -(-(row_line(16) - row_line(-6)) // 8)
    for which in range(3):
        reach = 3 * (2 - which)
        low_row, high_row = -reach, ROWS + reach
        first, last = row_line(low_row), row_line(high_row + 3) + 1
        if which:
            prepare_lines(state, row_line(low_row - 3), 5)
            if which == 2:
                copy.start()
            start, count = first, -(-(last - first) // 8)
            force_lines(state, start, count)
        last = row_line(high_row) + 1
        for line in range(start + 8 * count - LAG, last, 8):
            carry_lines(push, over, line)
        update_lines(state, first, -(-(last - first) // 8), which, (8, 8, 9)[which])
        if which:
            collected = (moved, vel_ref)[which - 1]
            for tile in range(ROWS):
                lines = pl.ds(row_line(0) + 1 + tile, ROWS, stride=PITCH)
                for part in range(2):
                    collected[part, :, pl.ds(tile * LANES, LANES)] = data[
                        2 * (which - 1) + part, lines, :
                    ]
    copy.wait()


def shift(array, axis, by):
    count = lax.axis_size(axis)
    return lax.ppermute(array, axis, [(i, (i + by) % count) for i in range(count)])


def swap(array, axis, odd):
    count = lax.axis_size(axis)
    pairs = []
    for i in range(odd, count + odd, 2):
        pairs += [(i % count, (i + 1) % count), ((i + 1) % count, i % count)]
    return lax.ppermute(array, axis, pairs)


VMEM = pl.BlockSpec(memory_space=pltpu.VMEM)


def per_device(disp, vel, bonds):
    f32 = jnp.float32
    small = pltpu.CompilerParams(vmem_limit_bytes=4 * 2**20)
    paced = pltpu.CompilerParams(
        vmem_limit_bytes=4 * 2**20,
    )
    edge, disp, vel, bonds = pl.pallas_call(
        edge_kernel,
        out_shape=(
            jax.ShapeDtypeStruct((8 * FIELDS, LANES), f32),
            jax.ShapeDtypeStruct(disp.shape, disp.dtype),
            jax.ShapeDtypeStruct(vel.shape, vel.dtype),
            jax.ShapeDtypeStruct(bonds.shape, bonds.dtype),
        ),
        in_specs=[pl.BlockSpec(memory_space=pltpu.HBM)] * 3,
        out_specs=(VMEM,) * 4,
        scratch_shapes=[pltpu.SemaphoreType.DMA((3,))],
        compiler_params=small,
        name="edge",
    )(*(pltpu.with_memory_space_constraint(x, pltpu.HBM) for x in (disp, vel, bonds)))
    odd_edge = swap(edge, "gy", 1)
    even_edge = swap(edge, "gy", 0)
    ends = jax.ShapeDtypeStruct((FIELDS * PITCH, LANES), f32)
    block, first, last = pl.pallas_call(
        block_kernel,
        out_shape=(jax.ShapeDtypeStruct((FIELDS * BLOCK, LANES), f32), ends, ends),
        in_specs=[VMEM] * 5,
        out_specs=(VMEM,) * 3,
        compiler_params=small,
        name="block",
    )(disp, vel, bonds, even_edge, odd_edge)
    odd_block = swap(block, "gx", 1)
    even_block = swap(block, "gx", 0)
    below = shift(last, "gx", 2)
    above = shift(first, "gx", -2)
    work = (
        jax.ShapeDtypeStruct((4, LINES, LANES), f32),
        jax.ShapeDtypeStruct((LINES, LANES), jnp.int32),
        jax.ShapeDtypeStruct((12, LINES, LANES), f32),
        jax.ShapeDtypeStruct((3, LINES, LANES), jnp.int32),
        jax.ShapeDtypeStruct((24, LINES, LANES), f32),
        jax.ShapeDtypeStruct((8, LINES, LANES), f32),
        jax.ShapeDtypeStruct((26, LINES, LANES), f32),
        jax.ShapeDtypeStruct((6, LINES, LANES), f32),
    )
    state = pl.pallas_call(
        first_kernel,
        out_shape=work,
        in_specs=[VMEM] * 4,
        out_specs=(VMEM,) * len(work),
        compiler_params=paced,
        cost_estimate=pl.CostEstimate(
            flops=20_000_000, bytes_accessed=8_000_000, transcendentals=500_000
        ),
        name="first",
    )(block, even_block, odd_block, below)
    out = jax.ShapeDtypeStruct(disp.shape, f32)
    results = pl.pallas_call(
        rest_kernel,
        out_shape=(out, out) + work,
        in_specs=[VMEM] * (1 + len(work)),
        out_specs=(pl.BlockSpec(memory_space=pltpu.HBM),) + (VMEM,) * (1 + len(work)),
        scratch_shapes=[
            pltpu.VMEM(disp.shape, f32),
            pltpu.SemaphoreType.DMA,
        ],
        input_output_aliases={1 + k: 2 + k for k in range(len(work))},
        compiler_params=paced,
        name="rest",
    )(above, *state)
    return results[0], results[1]


def solution(mesh):
    spec = P(None, "gx", "gy")
    return jax.shard_map(
        per_device,
        mesh=mesh,
        in_specs=(spec, spec, spec),
        out_specs=(spec, spec),
        check_vma=False,
    )
```

```python
import math

import jax
import jax.numpy as jnp
from jax import lax
from jax.experimental import pallas as pl
from jax.experimental.pallas import tpu as pltpu
from jax.sharding import PartitionSpec as P

STIFFNESS = 40.0
TIME_STEP = 0.05
SOFTENING = 0.0625
PACK_SHIFT = (0, 3, 10, 17)
LANES = 128

ROWS = 8
PITCH = 9
BLOCK = ROWS * PITCH
FIELDS = 5
HALO = 9
GUARD = 16
LINES = 280
LAG = 40


def row_line(row):
    return GUARD + PITCH * (row + HALO)


def lane_ids():
    return lax.broadcasted_iota(jnp.int32, (8, LANES), 1)


def edge_kernel(disp_hbm, vel_hbm, bonds_hbm, edge_ref, disp, vel, bonds, sems):
    copies = [
        pltpu.make_async_copy(source, target, sems.at[k])
        for k, (source, target) in enumerate(
            ((disp_hbm, disp), (vel_hbm, vel), (bonds_hbm, bonds))
        )
    ]
    for copy in copies:
        copy.start()
    for copy in copies:
        copy.wait()
    low_half = lane_ids() < LANES // 2
    left = pl.ds(0, LANES)
    right = pl.ds((ROWS - 1) * LANES, LANES)

    def ends(ref, part):
        return jnp.where(low_half, ref[part, :, left], ref[part, :, right])

    for part in range(2):
        edge_ref[pl.ds(8 * part, 8), :] = ends(disp, part)
        edge_ref[pl.ds(8 * part + 16, 8), :] = ends(vel, part)
    edge_ref[pl.ds(32, 8), :] = packed([ends(bonds, word) for word in range(4)])


def packed(words):
    total = words[0]
    for word in (1, 2, 3):
        total = total + words[word] * (1 << PACK_SHIFT[word])
    return total.astype(jnp.float32)


def block_kernel(disp_ref, vel_ref, bonds_ref, even_ref, odd_ref, block_ref, first_ref, last_ref):
    low_half = lane_ids() < LANES // 2
    is_even = lax.rem(lax.axis_index("gy"), 2) == 0
    for field in range(FIELDS):
        even = even_ref[pl.ds(8 * field, 8), :]
        odd = odd_ref[pl.ds(8 * field, 8), :]
        from_right = jnp.where(is_even, even, odd)
        from_left = jnp.where(is_even, odd, even)
        lines = [jnp.where(low_half, from_right, from_left)]
        for tile in range(ROWS):
            cols = pl.ds(tile * LANES, LANES)
            if field < 2:
                lines.append(disp_ref[field, :, cols])
            elif field < 4:
                lines.append(vel_ref[field - 2, :, cols])
            else:
                lines.append(packed([bonds_ref[word, :, cols] for word in range(4)]))
        for k, value in enumerate(lines):
            block_ref[pl.ds(field * BLOCK + k, ROWS, stride=PITCH), :] = value
            first_ref[pl.ds(PITCH * field + k, 1), :] = value[:1]
            last_ref[pl.ds(PITCH * field + k, 1), :] = value[7:]


def look_ahead(data, ahead, line, lanes):
    here = [data[f, pl.ds(line, 8), :] for f in range(4)]
    after = [data[f, pl.ds(line + 1, 8), :] for f in range(4)]
    for by in (1, 2, 3):
        for f in range(4):
            value = pltpu.roll(jnp.where(lanes < by, after[f], here[f]), LANES - by, 1)
            if f == 1:
                value = value + float(by)
            ahead[4 * (by - 1) + f, pl.ds(line, 8), :] = value


def prepare_lines(state, start, count):
    lanes = lane_ids()
    for step in range(count):
        look_ahead(state[0], state[2], start + 8 * step, lanes)


def mask_lines(state, start, count, ahead_start, ahead_count):
    _, words, _, ahead_words, masks = state[:5]
    lanes = lane_ids()
    for step in range(ahead_count):
        line = ahead_start + 8 * step
        here, after = words[pl.ds(line, 8), :], words[pl.ds(line + 1, 8), :]
        for by in (1, 2, 3):
            ahead_words[by - 1, pl.ds(line, 8), :] = pltpu.roll(
                jnp.where(lanes < by, after, here), LANES - by, 1
            )

    def fill(line):
        def mask(slot, row_off, col_off, word):
            weight = 1.0 / (row_off * row_off + col_off * col_off)
            return slot, jnp.where((word & (1 << slot)) != 0, weight, 0.0)

        made = []
        for row_off in range(4):
            word = words[pl.ds(line - PITCH * row_off, 8), :]
            for col_off in range(4):
                if row_off == 0:
                    if col_off:
                        made.append(mask(col_off - 1, row_off, col_off, word))
                    continue
                made.append(mask(PACK_SHIFT[row_off] + col_off + 3, row_off, col_off, word))
                if col_off:
                    far_word = ahead_words[col_off - 1, pl.ds(line - PITCH * row_off, 8), :]
                    slot = PACK_SHIFT[row_off] - col_off + 3
                    made.append(mask(slot, row_off, col_off, far_word))
        for slot, value in made:
            masks[slot, pl.ds(line, 8), :] = value

    def body(step, carry):
        for k in range(2):
            fill(start + 16 * step + 8 * k)
        return carry

    lax.fori_loop(0, -(-count // 2), body, 0)


def bond_pull(far, near, row_off, col_off, mask):
    rest = math.sqrt(row_off * row_off + col_off * col_off + SOFTENING)
    along_x = far[0] - near[0]
    along_y = far[1] - near[1]
    rate_x = far[2] - near[2]
    rate_y = far[3] - near[3]
    inverse = lax.rsqrt(along_x * along_x + (along_y * along_y + SOFTENING))
    dot = along_x * rate_x + along_y * rate_y
    scale = mask * (STIFFNESS - (STIFFNESS * rest - dot * inverse) * inverse)
    return (scale * along_x, scale * along_y)


def added(total, value):
    if total is None:
        return list(value)
    return [total[part] + value[part] for part in range(2)]


def force_lines(state, start, count, carrying=True):
    data, _, ahead, _, masks, pull, push, over = state
    lanes = lane_ids()

    def body(step, carry):
        line = start + 8 * step
        here = [data[f, pl.ds(line, 8), :] for f in range(4)]
        found = [[ahead[4 * b + f, pl.ds(line, 8), :] for f in range(4)] for b in range(3)]
        look_ahead(data, ahead, line + 8, lanes)
        if carrying:
            carry_lines(push, over, line - LAG)

        def at(ref, k, offset):
            return ref[k, pl.ds(line - PITCH * offset, 8), :]

        def store(ref, k, value):
            for part in range(2):
                ref[2 * k + part, pl.ds(line, 8), :] = value[part]

        own = [None] * 4
        reach = [None] * 4
        for row_off in range(4):
            near = here if row_off == 0 else [at(data, f, row_off) for f in range(4)]
            if row_off:
                near[0] = near[0] - float(row_off)
            for col_off in range(4):
                if row_off == 0 and col_off == 0:
                    continue
                far = found[col_off - 1] if col_off else here
                slot = col_off - 1 if row_off == 0 else PACK_SHIFT[row_off] + col_off + 3
                mask = masks[slot, pl.ds(line, 8), :]
                value = bond_pull(far, near, row_off, col_off, mask)
                own[row_off] = added(own[row_off], value)
                reach[col_off] = added(reach[col_off], value)
        for col_off in range(4):
            store(push, col_off, reach[col_off])
        for row_off in (1, 2, 3):
            near = [here[0] + float(row_off)] + list(here[1:])
            for col_off in (1, 2, 3):
                far = [at(ahead, 4 * (col_off - 1) + f, row_off) for f in range(4)]
                slot = PACK_SHIFT[row_off] - col_off + 3
                mask = masks[slot, pl.ds(line, 8), :]
                value = bond_pull(far, near, row_off, col_off, mask)
                own[0] = added(own[0], value)
                store(push, 3 * row_off + col_off, value)
        for row_off in range(4):
            store(pull, row_off, own[row_off])
        return carry

    lax.fori_loop(0, count, body, 0)


def carry_lines(push, over, line):
    for part in range(2):
        for col_off in (1, 2, 3):
            total = push[2 * col_off + part, pl.ds(line, 8), :]
            for row_off in (1, 2, 3):
                slot = 2 * (3 * row_off + col_off) + part
                total = total + push[slot, pl.ds(line + PITCH * row_off, 8), :]
            over[2 * (col_off - 1) + part, pl.ds(line, 8), :] = pltpu.roll(total, col_off, 1)


def update_lines(state, start, count, which, unroll):
    data, _, _, _, _, pull, push, over = state
    lanes = lane_ids()

    def gain_at(line, part):
        def at(ref, k, offset):
            return ref[2 * k + part, pl.ds(line + offset, 8), :]

        force = at(pull, 0, 0) - at(push, 0, 0)
        for row_off in (1, 2, 3):
            force = force + at(pull, row_off, PITCH * row_off)
        for k in range(3):
            force = force - jnp.where(lanes > k, at(over, k, 0), at(over, k, -1))
        return (0.5 * TIME_STEP) * force

    def body(step, carry):
        stores = []
        for k in range(unroll):
            line = start + 8 * unroll * step + 8 * k
            for part in range(2):
                gain = gain_at(line, part)
                speed = data[2 + part, pl.ds(line, 8), :] + gain
                if which == 1:
                    speed = speed + gain
                stores.append((2 + part, line, speed))
                if which < 2:
                    moved = data[part, pl.ds(line, 8), :] + TIME_STEP * speed
                    stores.append((part, line, moved))
        for field, line, value in stores:
            data[field, pl.ds(line, 8), :] = value
        return carry

    lax.fori_loop(0, -(-count // unroll), body, 0)


def first_kernel(block_ref, even_ref, odd_ref, below_ref, *state):
    data, words = state[:2]
    low_half = lane_ids() < LANES // 2
    is_even = lax.rem(lax.axis_index("gx"), 2) == 0
    even_line = jnp.where(is_even, row_line(8), row_line(-8))
    odd_line = jnp.where(is_even, row_line(-8), row_line(8))

    def get(field, lines):
        return data[field, lines, :] if field < 4 else words[lines, :]

    def put(field, lines, value):
        if field < 4:
            data[field, lines, :] = value
        else:
            words[lines, :] = value

    for field in range(FIELDS):
        for part in range(PITCH):
            source = pl.ds(field * BLOCK + 8 * part, 8)
            for ref, line in (
                (block_ref, row_line(0)), (even_ref, even_line), (odd_ref, odd_line)
            ):
                value = ref[source, :]
                if field == 4:
                    value = value.astype(jnp.int32)
                put(field, pl.ds(line + 8 * part, 8), value)
        value = below_ref[pl.ds(PITCH * field, PITCH), :]
        if field == 4:
            value = value.astype(jnp.int32)
        put(field, pl.ds(row_line(-9), PITCH), value)
    for field in range(FIELDS):
        firsts = [row_line(row) for row in (-8, 0, 8)]
        heads = [get(field, pl.ds(line, 8, stride=PITCH)) for line in firsts]
        below = [get(field, pl.ds(line - PITCH, 8, stride=PITCH)) for line in firsts]
        final = get(field, pl.ds(row_line(15), 1))
        for line, head, last in zip(firsts, heads, below):
            put(field, pl.ds(line, 8, stride=PITCH), jnp.where(low_half, last, head))
        put(field, pl.ds(row_line(16), 1), final)
    first, last = row_line(-6), row_line(16)
    count = -(-(last - first) // 8)
    mask_lines(state, first, count, row_line(-9), 28)
    prepare_lines(state, row_line(-9), 5)
    force_lines(state, first, count)


def rest_kernel(above_ref, *refs):
    state_count = (len(refs) - 2) // 2
    disp_ref, vel_ref = refs[state_count : state_count + 2]
    state = refs[state_count + 2 :]
    data, words = state[:2]
    push, over = state[6:]
    low = lax.broadcasted_iota(jnp.int32, (1, LANES), 1) < LANES // 2
    for field in range(FIELDS):
        above = above_ref[pl.ds(PITCH * field, PITCH), :]
        if field == 4:
            above = above.astype(jnp.int32)
        target = data.at[field] if field < 4 else words
        head = pl.ds(row_line(16), 1)
        kept = target[head, :]
        target[pl.ds(row_line(16), PITCH), :] = above
        target[head, :] = jnp.where(low, kept, above[:1])
        target[pl.ds(row_line(17), 1), :] = above[:1]
    mask_lines(state, row_line(16), 2, row_line(16) - 1, 1)
    prepare_lines(state, row_line(16), 1)
    force_lines(state, row_line(16), 2, False)
    start, count = row_line(-6), -(-(row_line(16) - row_line(-6)) // 8)
    for which in range(3):
        reach = 3 * (2 - which)
        low_row, high_row = -reach, ROWS + reach
        first, last = row_line(low_row), row_line(high_row + 3) + 1
        if which:
            prepare_lines(state, row_line(low_row - 3), 5)
            start, count = first, -(-(last - first) // 8)
            force_lines(state, start, count)
        last = row_line(high_row) + 1
        for line in range(start + 8 * count - LAG, last, 8):
            carry_lines(push, over, line)
        update_lines(state, first, -(-(last - first) // 8), which, (8, 8, 9)[which])
    for tile in range(ROWS):
        lines = pl.ds(row_line(0) + 1 + tile, ROWS, stride=PITCH)
        cols = pl.ds(tile * LANES, LANES)
        for part in range(2):
            disp_ref[part, :, cols] = data[part, lines, :]
            vel_ref[part, :, cols] = data[2 + part, lines, :]


def shift(array, axis, by):
    count = lax.axis_size(axis)
    return lax.ppermute(array, axis, [(i, (i + by) % count) for i in range(count)])


def swap(array, axis, odd):
    count = lax.axis_size(axis)
    pairs = []
    for i in range(odd, count + odd, 2):
        pairs += [(i % count, (i + 1) % count), ((i + 1) % count, i % count)]
    return lax.ppermute(array, axis, pairs)


VMEM = pl.BlockSpec(memory_space=pltpu.VMEM)


def per_device(disp, vel, bonds):
    f32 = jnp.float32
    small = pltpu.CompilerParams(vmem_limit_bytes=4 * 2**20)
    paced = pltpu.CompilerParams(
        vmem_limit_bytes=4 * 2**20,
    )
    edge, disp, vel, bonds = pl.pallas_call(
        edge_kernel,
        out_shape=(
            jax.ShapeDtypeStruct((8 * FIELDS, LANES), f32),
            jax.ShapeDtypeStruct(disp.shape, disp.dtype),
            jax.ShapeDtypeStruct(vel.shape, vel.dtype),
            jax.ShapeDtypeStruct(bonds.shape, bonds.dtype),
        ),
        in_specs=[pl.BlockSpec(memory_space=pltpu.HBM)] * 3,
        out_specs=(VMEM,) * 4,
        scratch_shapes=[pltpu.SemaphoreType.DMA((3,))],
        compiler_params=small,
        name="edge",
    )(*(pltpu.with_memory_space_constraint(x, pltpu.HBM) for x in (disp, vel, bonds)))
    odd_edge = swap(edge, "gy", 1)
    even_edge = swap(edge, "gy", 0)
    ends = jax.ShapeDtypeStruct((FIELDS * PITCH, LANES), f32)
    block, first, last = pl.pallas_call(
        block_kernel,
        out_shape=(jax.ShapeDtypeStruct((FIELDS * BLOCK, LANES), f32), ends, ends),
        in_specs=[VMEM] * 5,
        out_specs=(VMEM,) * 3,
        compiler_params=small,
        name="block",
    )(disp, vel, bonds, even_edge, odd_edge)
    odd_block = swap(block, "gx", 1)
    even_block = swap(block, "gx", 0)
    below = shift(last, "gx", 2)
    above = shift(first, "gx", -2)
    work = (
        jax.ShapeDtypeStruct((4, LINES, LANES), f32),
        jax.ShapeDtypeStruct((LINES, LANES), jnp.int32),
        jax.ShapeDtypeStruct((12, LINES, LANES), f32),
        jax.ShapeDtypeStruct((3, LINES, LANES), jnp.int32),
        jax.ShapeDtypeStruct((24, LINES, LANES), f32),
        jax.ShapeDtypeStruct((8, LINES, LANES), f32),
        jax.ShapeDtypeStruct((26, LINES, LANES), f32),
        jax.ShapeDtypeStruct((6, LINES, LANES), f32),
    )
    state = pl.pallas_call(
        first_kernel,
        out_shape=work,
        in_specs=[VMEM] * 4,
        out_specs=(VMEM,) * len(work),
        compiler_params=paced,
        cost_estimate=pl.CostEstimate(
            flops=20_000_000, bytes_accessed=8_000_000, transcendentals=500_000
        ),
        name="first",
    )(block, even_block, odd_block, below)
    out = jax.ShapeDtypeStruct(disp.shape, f32)
    results = pl.pallas_call(
        rest_kernel,
        out_shape=(out, out) + work,
        in_specs=[VMEM] * (1 + len(work)),
        out_specs=(VMEM,) * (2 + len(work)),
        input_output_aliases={1 + k: 2 + k for k in range(len(work))},
        compiler_params=paced,
        name="rest",
    )(above, *state)
    return results[0], results[1]


def solution(mesh):
    spec = P(None, "gx", "gy")
    return jax.shard_map(
        per_device,
        mesh=mesh,
        in_specs=(spec, spec, spec),
        out_specs=(spec, spec),
        check_vma=False,
    )
```

```python
import math

import jax
import jax.numpy as jnp
from jax import lax
from jax.experimental import pallas as pl
from jax.experimental.pallas import tpu as pltpu
from jax.sharding import PartitionSpec as P

STIFFNESS = 40.0
TIME_STEP = 0.05
SOFTENING = 0.0625
PACK_SHIFT = (0, 3, 10, 17)
LANES = 128

ROWS = 8
PITCH = 9
BLOCK = ROWS * PITCH
FIELDS = 5
HALO = 9
GUARD = 16
LINES = 280
LAG = 40


def row_line(row):
    return GUARD + PITCH * (row + HALO)


def lane_ids():
    return lax.broadcasted_iota(jnp.int32, (8, LANES), 1)


def edge_kernel(disp_hbm, vel_hbm, bonds_hbm, edge_ref, disp, vel, bonds, sems):
    copies = [
        pltpu.make_async_copy(source, target, sems.at[k])
        for k, (source, target) in enumerate(
            ((disp_hbm, disp), (vel_hbm, vel), (bonds_hbm, bonds))
        )
    ]
    for copy in copies:
        copy.start()
    low_half = lane_ids() < LANES // 2
    left = pl.ds(0, LANES)
    right = pl.ds((ROWS - 1) * LANES, LANES)

    def ends(ref, part):
        return jnp.where(low_half, ref[part, :, left], ref[part, :, right])

    for k, ref in enumerate((disp, vel)):
        copies[k].wait()
        for part in range(2):
            edge_ref[pl.ds(16 * k + 8 * part, 8), :] = ends(ref, part)
    copies[2].wait()
    edge_ref[pl.ds(32, 8), :] = packed([ends(bonds, word) for word in range(4)])


def packed(words):
    total = words[0]
    for word in (1, 2, 3):
        total = total + words[word] * (1 << PACK_SHIFT[word])
    return total.astype(jnp.float32)


def block_kernel(disp_ref, vel_ref, bonds_ref, even_ref, odd_ref, block_ref, first_ref, last_ref):
    low_half = lane_ids() < LANES // 2
    is_even = lax.rem(lax.axis_index("gy"), 2) == 0
    for field in range(FIELDS):
        even = even_ref[pl.ds(8 * field, 8), :]
        odd = odd_ref[pl.ds(8 * field, 8), :]
        from_right = jnp.where(is_even, even, odd)
        from_left = jnp.where(is_even, odd, even)
        lines = [jnp.where(low_half, from_right, from_left)]
        for tile in range(ROWS):
            cols = pl.ds(tile * LANES, LANES)
            if field < 2:
                lines.append(disp_ref[field, :, cols])
            elif field < 4:
                lines.append(vel_ref[field - 2, :, cols])
            else:
                lines.append(packed([bonds_ref[word, :, cols] for word in range(4)]))
        for k, value in enumerate(lines):
            block_ref[pl.ds(field * BLOCK + k, ROWS, stride=PITCH), :] = value
            first_ref[pl.ds(PITCH * field + k, 1), :] = value[:1]
            last_ref[pl.ds(PITCH * field + k, 1), :] = value[7:]


def look_ahead(data, ahead, line, lanes):
    here = [data[f, pl.ds(line, 8), :] for f in range(4)]
    after = [data[f, pl.ds(line + 1, 8), :] for f in range(4)]
    for by in (1, 2, 3):
        for f in range(4):
            value = pltpu.roll(jnp.where(lanes < by, after[f], here[f]), LANES - by, 1)
            if f == 1:
                value = value + float(by)
            ahead[4 * (by - 1) + f, pl.ds(line, 8), :] = value


def prepare_lines(state, start, count):
    lanes = lane_ids()
    for step in range(count):
        look_ahead(state[0], state[2], start + 8 * step, lanes)


def mask_lines(state, start, count, ahead_start, ahead_count):
    _, words, _, ahead_words, masks = state[:5]
    lanes = lane_ids()
    for step in range(ahead_count):
        line = ahead_start + 8 * step
        here, after = words[pl.ds(line, 8), :], words[pl.ds(line + 1, 8), :]
        for by in (1, 2, 3):
            ahead_words[by - 1, pl.ds(line, 8), :] = pltpu.roll(
                jnp.where(lanes < by, after, here), LANES - by, 1
            )

    def fill(line):
        def mask(slot, row_off, col_off, word):
            weight = 1.0 / (row_off * row_off + col_off * col_off)
            return slot, jnp.where((word & (1 << slot)) != 0, weight, 0.0)

        made = []
        for row_off in range(4):
            word = words[pl.ds(line - PITCH * row_off, 8), :]
            for col_off in range(4):
                if row_off == 0:
                    if col_off:
                        made.append(mask(col_off - 1, row_off, col_off, word))
                    continue
                made.append(mask(PACK_SHIFT[row_off] + col_off + 3, row_off, col_off, word))
                if col_off:
                    far_word = ahead_words[col_off - 1, pl.ds(line - PITCH * row_off, 8), :]
                    slot = PACK_SHIFT[row_off] - col_off + 3
                    made.append(mask(slot, row_off, col_off, far_word))
        for slot, value in made:
            masks[slot, pl.ds(line, 8), :] = value

    def body(step, carry):
        for k in range(2):
            fill(start + 16 * step + 8 * k)
        return carry

    lax.fori_loop(0, -(-count // 2), body, 0)


def bond_pull(far, near, row_off, col_off, mask):
    rest = math.sqrt(row_off * row_off + col_off * col_off + SOFTENING)
    along_x = far[0] - near[0]
    along_y = far[1] - near[1]
    rate_x = far[2] - near[2]
    rate_y = far[3] - near[3]
    inverse = lax.rsqrt(along_x * along_x + (along_y * along_y + SOFTENING))
    dot = along_x * rate_x + along_y * rate_y
    scale = mask * (STIFFNESS - (STIFFNESS * rest - dot * inverse) * inverse)
    return (scale * along_x, scale * along_y)


def added(total, value):
    if total is None:
        return list(value)
    return [total[part] + value[part] for part in range(2)]


def force_lines(state, start, count, carrying=True):
    data, _, ahead, _, masks, pull, push, over = state
    lanes = lane_ids()

    def body(step, carry):
        line = start + 8 * step
        here = [data[f, pl.ds(line, 8), :] for f in range(4)]
        found = [[ahead[4 * b + f, pl.ds(line, 8), :] for f in range(4)] for b in range(3)]
        look_ahead(data, ahead, line + 8, lanes)
        if carrying:
            carry_lines(push, over, line - LAG)

        def at(ref, k, offset):
            return ref[k, pl.ds(line - PITCH * offset, 8), :]

        def store(ref, k, value):
            for part in range(2):
                ref[2 * k + part, pl.ds(line, 8), :] = value[part]

        own = [None] * 4
        reach = [None] * 4
        for row_off in range(4):
            near = here if row_off == 0 else [at(data, f, row_off) for f in range(4)]
            if row_off:
                near[0] = near[0] - float(row_off)
            for col_off in range(4):
                if row_off == 0 and col_off == 0:
                    continue
                far = found[col_off - 1] if col_off else here
                slot = col_off - 1 if row_off == 0 else PACK_SHIFT[row_off] + col_off + 3
                mask = masks[slot, pl.ds(line, 8), :]
                value = bond_pull(far, near, row_off, col_off, mask)
                own[row_off] = added(own[row_off], value)
                reach[col_off] = added(reach[col_off], value)
        for col_off in range(4):
            store(push, col_off, reach[col_off])
        for row_off in (1, 2, 3):
            near = [here[0] + float(row_off)] + list(here[1:])
            for col_off in (1, 2, 3):
                far = [at(ahead, 4 * (col_off - 1) + f, row_off) for f in range(4)]
                slot = PACK_SHIFT[row_off] - col_off + 3
                mask = masks[slot, pl.ds(line, 8), :]
                value = bond_pull(far, near, row_off, col_off, mask)
                own[0] = added(own[0], value)
                store(push, 3 * row_off + col_off, value)
        for row_off in range(4):
            store(pull, row_off, own[row_off])
        return carry

    lax.fori_loop(0, count, body, 0)


def carry_lines(push, over, line):
    for part in range(2):
        for col_off in (1, 2, 3):
            total = push[2 * col_off + part, pl.ds(line, 8), :]
            for row_off in (1, 2, 3):
                slot = 2 * (3 * row_off + col_off) + part
                total = total + push[slot, pl.ds(line + PITCH * row_off, 8), :]
            over[2 * (col_off - 1) + part, pl.ds(line, 8), :] = pltpu.roll(total, col_off, 1)


def update_lines(state, start, count, which, unroll):
    data, _, _, _, _, pull, push, over = state
    lanes = lane_ids()

    def gain_at(line, part):
        def at(ref, k, offset):
            return ref[2 * k + part, pl.ds(line + offset, 8), :]

        force = at(pull, 0, 0) - at(push, 0, 0)
        for row_off in (1, 2, 3):
            force = force + at(pull, row_off, PITCH * row_off)
        for k in range(3):
            force = force - jnp.where(lanes > k, at(over, k, 0), at(over, k, -1))
        return (0.5 * TIME_STEP) * force

    def body(step, carry):
        stores = []
        for k in range(unroll):
            line = start + 8 * unroll * step + 8 * k
            for part in range(2):
                gain = gain_at(line, part)
                speed = data[2 + part, pl.ds(line, 8), :] + gain
                if which == 1:
                    speed = speed + gain
                stores.append((2 + part, line, speed))
                if which < 2:
                    moved = data[part, pl.ds(line, 8), :] + TIME_STEP * speed
                    stores.append((part, line, moved))
        for field, line, value in stores:
            data[field, pl.ds(line, 8), :] = value
        return carry

    lax.fori_loop(0, -(-count // unroll), body, 0)


def first_kernel(block_ref, even_ref, odd_ref, below_ref, *state):
    data, words = state[:2]
    low_half = lane_ids() < LANES // 2
    is_even = lax.rem(lax.axis_index("gx"), 2) == 0
    even_line = jnp.where(is_even, row_line(8), row_line(-8))
    odd_line = jnp.where(is_even, row_line(-8), row_line(8))

    def get(field, lines):
        return data[field, lines, :] if field < 4 else words[lines, :]

    def put(field, lines, value):
        if field < 4:
            data[field, lines, :] = value
        else:
            words[lines, :] = value

    for field in range(FIELDS):
        for part in range(PITCH):
            source = pl.ds(field * BLOCK + 8 * part, 8)
            for ref, line in (
                (block_ref, row_line(0)), (even_ref, even_line), (odd_ref, odd_line)
            ):
                value = ref[source, :]
                if field == 4:
                    value = value.astype(jnp.int32)
                put(field, pl.ds(line + 8 * part, 8), value)
        value = below_ref[pl.ds(PITCH * field, PITCH), :]
        if field == 4:
            value = value.astype(jnp.int32)
        put(field, pl.ds(row_line(-9), PITCH), value)
    for field in range(FIELDS):
        firsts = [row_line(row) for row in (-8, 0, 8)]
        heads = [get(field, pl.ds(line, 8, stride=PITCH)) for line in firsts]
        below = [get(field, pl.ds(line - PITCH, 8, stride=PITCH)) for line in firsts]
        final = get(field, pl.ds(row_line(15), 1))
        for line, head, last in zip(firsts, heads, below):
            put(field, pl.ds(line, 8, stride=PITCH), jnp.where(low_half, last, head))
        put(field, pl.ds(row_line(16), 1), final)
    first, last = row_line(-6), row_line(16)
    count = -(-(last - first) // 8)
    mask_lines(state, first, count, row_line(-9), 28)
    prepare_lines(state, row_line(-9), 5)
    force_lines(state, first, count)


def rest_kernel(above_ref, *refs):
    state_count = (len(refs) - 2) // 2
    disp_ref, vel_ref = refs[state_count : state_count + 2]
    state = refs[state_count + 2 :]
    data, words = state[:2]
    push, over = state[6:]
    low = lax.broadcasted_iota(jnp.int32, (1, LANES), 1) < LANES // 2
    for field in range(FIELDS):
        above = above_ref[pl.ds(PITCH * field, PITCH), :]
        if field == 4:
            above = above.astype(jnp.int32)
        target = data.at[field] if field < 4 else words
        head = pl.ds(row_line(16), 1)
        kept = target[head, :]
        target[pl.ds(row_line(16), PITCH), :] = above
        target[head, :] = jnp.where(low, kept, above[:1])
        target[pl.ds(row_line(17), 1), :] = above[:1]
    mask_lines(state, row_line(16), 2, row_line(16) - 1, 1)
    prepare_lines(state, row_line(16), 1)
    force_lines(state, row_line(16), 2, False)
    start, count = row_line(-6), -(-(row_line(16) - row_line(-6)) // 8)
    for which in range(3):
        reach = 3 * (2 - which)
        low_row, high_row = -reach, ROWS + reach
        first, last = row_line(low_row), row_line(high_row + 3) + 1
        if which:
            prepare_lines(state, row_line(low_row - 3), 5)
            start, count = first, -(-(last - first) // 8)
            force_lines(state, start, count)
        last = row_line(high_row) + 1
        for line in range(start + 8 * count - LAG, last, 8):
            carry_lines(push, over, line)
        update_lines(state, first, -(-(last - first) // 8), which, (8, 8, 9)[which])
    for tile in range(ROWS):
        lines = pl.ds(row_line(0) + 1 + tile, ROWS, stride=PITCH)
        cols = pl.ds(tile * LANES, LANES)
        for part in range(2):
            disp_ref[part, :, cols] = data[part, lines, :]
            vel_ref[part, :, cols] = data[2 + part, lines, :]


def shift(array, axis, by):
    count = lax.axis_size(axis)
    return lax.ppermute(array, axis, [(i, (i + by) % count) for i in range(count)])


def swap(array, axis, odd):
    count = lax.axis_size(axis)
    pairs = []
    for i in range(odd, count + odd, 2):
        pairs += [(i % count, (i + 1) % count), ((i + 1) % count, i % count)]
    return lax.ppermute(array, axis, pairs)


VMEM = pl.BlockSpec(memory_space=pltpu.VMEM)


def per_device(disp, vel, bonds):
    f32 = jnp.float32
    small = pltpu.CompilerParams(vmem_limit_bytes=4 * 2**20)
    paced = pltpu.CompilerParams(
        vmem_limit_bytes=4 * 2**20,
    )
    edge, disp, vel, bonds = pl.pallas_call(
        edge_kernel,
        out_shape=(
            jax.ShapeDtypeStruct((8 * FIELDS, LANES), f32),
            jax.ShapeDtypeStruct(disp.shape, disp.dtype),
            jax.ShapeDtypeStruct(vel.shape, vel.dtype),
            jax.ShapeDtypeStruct(bonds.shape, bonds.dtype),
        ),
        in_specs=[pl.BlockSpec(memory_space=pltpu.HBM)] * 3,
        out_specs=(VMEM,) * 4,
        scratch_shapes=[pltpu.SemaphoreType.DMA((3,))],
        compiler_params=small,
        name="edge",
    )(*(pltpu.with_memory_space_constraint(x, pltpu.HBM) for x in (disp, vel, bonds)))
    odd_edge = swap(edge, "gy", 1)
    even_edge = swap(edge, "gy", 0)
    ends = jax.ShapeDtypeStruct((FIELDS * PITCH, LANES), f32)
    block, first, last = pl.pallas_call(
        block_kernel,
        out_shape=(jax.ShapeDtypeStruct((FIELDS * BLOCK, LANES), f32), ends, ends),
        in_specs=[VMEM] * 5,
        out_specs=(VMEM,) * 3,
        compiler_params=small,
        name="block",
    )(disp, vel, bonds, even_edge, odd_edge)
    odd_block = swap(block, "gx", 1)
    even_block = swap(block, "gx", 0)
    below = shift(last, "gx", 2)
    above = shift(first, "gx", -2)
    work = (
        jax.ShapeDtypeStruct((4, LINES, LANES), f32),
        jax.ShapeDtypeStruct((LINES, LANES), jnp.int32),
        jax.ShapeDtypeStruct((12, LINES, LANES), f32),
        jax.ShapeDtypeStruct((3, LINES, LANES), jnp.int32),
        jax.ShapeDtypeStruct((24, LINES, LANES), f32),
        jax.ShapeDtypeStruct((8, LINES, LANES), f32),
        jax.ShapeDtypeStruct((26, LINES, LANES), f32),
        jax.ShapeDtypeStruct((6, LINES, LANES), f32),
    )
    state = pl.pallas_call(
        first_kernel,
        out_shape=work,
        in_specs=[VMEM] * 4,
        out_specs=(VMEM,) * len(work),
        compiler_params=paced,
        cost_estimate=pl.CostEstimate(
            flops=20_000_000, bytes_accessed=8_000_000, transcendentals=500_000
        ),
        name="first",
    )(block, even_block, odd_block, below)
    out = jax.ShapeDtypeStruct(disp.shape, f32)
    results = pl.pallas_call(
        rest_kernel,
        out_shape=(out, out) + work,
        in_specs=[VMEM] * (1 + len(work)),
        out_specs=(VMEM,) * (2 + len(work)),
        input_output_aliases={1 + k: 2 + k for k in range(len(work))},
        compiler_params=paced,
        name="rest",
    )(above, *state)
    return results[0], results[1]


def solution(mesh):
    spec = P(None, "gx", "gy")
    return jax.shard_map(
        per_device,
        mesh=mesh,
        in_specs=(spec, spec, spec),
        out_specs=(spec, spec),
        check_vma=False,
    )
```
